128 devices in a mesh: row: 32 (over z, y, core), sub: 4 (over x).
Axes of the slice: x: 4, y: 4, z: 4, core: 2. Of those that a mesh axis runs over, the one named last changes fastest.
Arguments:
- images: bfloat16 [32768, 3072], P(('row', 'sub')), may hold values from -6 to 6
- block_id: int32 [128, 32], replicated, may hold values from 0 to 4095, as said below
- panel_index: int32 [1], replicated, may hold values from 0 to 30
Outputs:
- factor_panel: float32 [32768, 1024], P(('row', 'sub'))
- next_panel: float32 [32768, 1024], P(('row', 'sub'))
The draws below stay inside these ranges and needn't reach their ends.
Inputs may be any that keep to these rules, and one draw needn't show every extreme that they name: `block_id`: column r holds r * 128 plus a permutation of 0 to 127, so every device stores exactly one block of every panel.
All inputs are finite; a program needn't handle non-finite values.
Results may differ from the reference program's by a relative error of at most 0.0015.
Values may be sent and summed in bfloat16 or wider, within the bound.
A program may use at most 128 MiB of HBM per device.

```python
import math
import jax
import jax.numpy as jnp
from jax import lax

F = 3072
PANEL = 1024
DEPTH = 10
R_DEV = 256
SHARDS = 128
GROUP = 8
ROUNDS = 32
IMAGES = 32768


def draw_block_id(key, part):
    rounds_all = jnp.arange(ROUNDS, dtype=jnp.int32)
    shuffled = jax.vmap(lambda which: jax.random.permutation(jax.random.fold_in(key, which), SHARDS))(rounds_all)
    return (shuffled.T + rounds_all[None, :] * SHARDS).astype(jnp.int32)


def level_of(stream_key, dims, cuts, least, high):
    loudness, own = 1.0, jax.random.fold_in(stream_key, 6)
    for axis_at, blocks in cuts:
        steps = jnp.exp(jax.random.uniform(jax.random.fold_in(own, axis_at), (blocks,), jnp.float32, least / len(cuts), high / len(cuts)))
        loudness = loudness * jnp.repeat(steps, dims[axis_at] // blocks).reshape([-1 if axis == axis_at else 1 for axis in range(len(dims))])
    return loudness


def bell_draw(rng, extent, scale, bound, pieces=(), held_as=jnp.bfloat16):
    drawn = scale * jax.random.normal(rng, extent, jnp.float32)
    if pieces:
        drawn = drawn * level_of(rng, extent, pieces, -0.22, 0.18)
    return jnp.clip(drawn, -bound, bound).astype(held_as)


def setup_inputs(seed: int = 0) -> dict:
    seeds = jax.random.split(jax.random.key(seed), 4)
    return {
        "images": bell_draw(seeds[0], (IMAGES, F), 1.0, 6.0, ((0, 128),)),
        "block_id": draw_block_id(jax.random.fold_in(seeds[3], 71), 0),
        "panel_index": jax.random.randint(seeds[2], (1,), 0, ROUNDS - 1).astype(jnp.int32),
    }


weight_var = 2.0
bias_var = 0.1
noise_var = 0.1

def base_kernel(left, right):
    gram = lax.dot_general(left.astype(jnp.float32), right.astype(jnp.float32), (((1,), (1,)), ((), ())), preferred_element_type=jnp.float32)
    return gram * (weight_var / left.shape[1]) + bias_var

def row_variance(rows):
    values = rows.astype(jnp.float32)
    return lax.optimization_barrier(jnp.sum(values * values, axis=1)) * (weight_var / rows.shape[1]) + bias_var

def relu_layers(kernel, left_var, right_var):

    def one_layer(step_index, carried):
        current, lvar, rvar = carried
        scales = jnp.sqrt(lvar[:, None] * rvar[None, :])
        cosine = jnp.clip(current / scales, -1.0, 1.0)
        angles = jnp.arccos(cosine)
        current = weight_var / (2.0 * math.pi) * scales * (jnp.sin(angles) + (math.pi - angles) * cosine) + bias_var
        return (current, 0.5 * weight_var * lvar + bias_var, 0.5 * weight_var * rvar + bias_var)
    return lax.fori_loop(0, DEPTH, one_layer, (kernel, left_var, right_var))[0]

def cross_kernel(left, right):
    return relu_layers(base_kernel(left, right), row_variance(left), row_variance(right))

def product_nt(left, right):
    return lax.dot_general(left.astype(jnp.float32), right.astype(jnp.float32), (((1,), (1,)), ((), ())), precision=lax.Precision.HIGHEST, preferred_element_type=jnp.float32)

def reference(images, block_id, panel_index):
    panel = panel_index[0]
    offsets = jnp.arange(GROUP, dtype=jnp.int32)
    global_rows = (block_id[:, :, None] * GROUP + offsets[None, None, :]).reshape(IMAGES).astype(jnp.int32)
    inverse_map = jnp.zeros((IMAGES,), jnp.int32).at[global_rows].set(jnp.arange(IMAGES, dtype=jnp.int32))
    panel_start = (panel * PANEL).astype(jnp.int32)
    next_start = panel_start + PANEL
    panel_images = images[lax.dynamic_slice_in_dim(inverse_map, panel_start, PANEL)]
    next_images = images[lax.dynamic_slice_in_dim(inverse_map, next_start, PANEL)]
    columns = jnp.arange(PANEL, dtype=jnp.int32)
    identity = jnp.eye(PANEL, dtype=jnp.float32)
    diagonal_block = cross_kernel(panel_images, panel_images) + noise_var * identity
    lower = jnp.linalg.cholesky(diagonal_block)
    inverse_factor = jax.scipy.linalg.solve_triangular(lower, identity, lower=True)
    next_factor = product_nt(cross_kernel(next_images, panel_images), inverse_factor)

    def one_slab(slab):
        rows, where_global = slab
        own_panel = (where_global[:, None] == panel_start + columns[None, :]).astype(jnp.float32)
        matrix = cross_kernel(rows, panel_images) + noise_var * own_panel
        solved = product_nt(matrix, inverse_factor)
        placed = lower[jnp.clip(where_global - panel_start, 0, PANEL - 1)]
        factor = jnp.where((where_global >= next_start)[:, None], solved, jnp.where((where_global >= panel_start)[:, None], placed, 0.0))
        own_next = (where_global[:, None] == next_start + columns[None, :]).astype(jnp.float32)
        updated = cross_kernel(rows, next_images) + noise_var * own_next - product_nt(factor, next_factor)
        updated = jnp.where((where_global >= next_start)[:, None], updated, 0.0)
        return (factor, updated)
    factor, updated = lax.map(one_slab, (images.reshape(SHARDS, R_DEV, F), global_rows.reshape(SHARDS, R_DEV)))
    return (factor.reshape(IMAGES, PANEL), updated.reshape(IMAGES, PANEL))
```

```python
import math

import jax
import jax.numpy as jnp
from jax import lax
from jax.experimental import pallas as pl
from jax.experimental.pallas import tpu as pltpu
from jax.sharding import PartitionSpec as P

PANEL = 1024
DEPTH = 10
GROUP = 8
TILE = 128
STEPS = PANEL // TILE

weight_var = 2.0
bias_var = 0.1
noise_var = 0.1
f32 = jnp.float32
bf16 = jnp.bfloat16

ARC = (
    0.30010470747947693,
    0.015018727630376816,
    0.0023307923693209887,
    0.0007760883891023695,
    -0.00012745900312438607,
    0.00020702359324786812,
)


def nn(a, b):
    return lax.dot_general(a, b, (((1,), (0,)), ((), ())), preferred_element_type=f32)


def nt(a, b):
    return lax.dot_general(a, b, (((1,), (1,)), ((), ())), preferred_element_type=f32)


def split3(x):
    h = x.astype(bf16)
    r = x - h.astype(f32)
    m = r.astype(bf16)
    l = (r - m.astype(f32)).astype(bf16)
    return h, m, l


def lhs6(x):
    h, m, l = split3(x)
    return jnp.concatenate([h, m, h, m, h, l], 1)


def rhs6_nn(x):
    h, m, l = split3(x)
    return jnp.concatenate([h, h, m, m, l, h], 0)


def rhs6_nt(x):
    h, m, l = split3(x)
    return jnp.concatenate([h, h, m, m, l, h], 1)


def own_square(rows_ref, start):
    rows = rows_ref[start : start + TILE, :]
    gram = nt(rows, rows)
    eye = lax.broadcasted_iota(jnp.int32, (TILE, TILE), 0) == lax.broadcasted_iota(
        jnp.int32, (TILE, TILE), 1
    )
    only = jnp.where(eye, gram, 0.0)
    scale = weight_var / rows_ref.shape[1]
    return (
        jnp.sum(only, axis=0, keepdims=True) * scale + bias_var,
        jnp.sum(only, axis=1, keepdims=True) * scale + bias_var,
    )


def layer_scales(q):
    inv = [lax.rsqrt(q + bias_var * n) for n in range(DEPTH)]
    ratio = [(q + bias_var * n) * inv[n] * inv[n + 1] for n in range(DEPTH - 1)]
    offset = [inv[n + 1] * math.sqrt(bias_var) for n in range(DEPTH - 1)]
    last = (q + bias_var * (DEPTH - 1)) * inv[DEPTH - 1]
    return inv[0], ratio, offset, last


def store_columns(tab_ref, start, q):
    first, ratio, offset, last = layer_scales(q)
    for at, row in enumerate([first] + ratio + offset + [last]):
        tab_ref[at : at + 1, start : start + TILE] = row


def relu_layers(gram, q_rows, tab_ref, lo, width):
    first, ratio, offset, last = layer_scales(q_rows)
    pieces = width // TILE
    col = lambda at, w: jnp.broadcast_to(
        tab_ref[at : at + 1, lo + w * TILE : lo + (w + 1) * TILE], (GROUP, TILE)
    )
    scale = weight_var / 3072
    c = [
        (gram[:, w * TILE : (w + 1) * TILE] * scale + bias_var) * (first * col(0, w))
        for w in range(pieces)
    ]
    for n in range(DEPTH):
        for w in range(pieces):
            u = jnp.maximum(1.0 - jnp.abs(c[w]), 1e-30)
            p = ARC[5] * u + ARC[4]
            for k in (3, 2, 1, 0):
                p = p * u + ARC[k]
            g = jnp.maximum(c[w], 0.0) + (u * u) * lax.rsqrt(u) * p
            if n < DEPTH - 1:
                c[w] = g * (ratio[n] * col(1 + n, w)) + offset[n] * col(DEPTH + n, w)
            else:
                c[w] = g * (last * col(2 * DEPTH - 1, w)) + bias_var
    return jnp.concatenate(c, axis=1)


def block_inverse(d_ref):
    lane = lax.broadcasted_iota(jnp.int32, (8, TILE), 1)
    sub = lax.broadcasted_iota(jnp.int32, (8, TILE), 0)
    spread = lambda x: jnp.broadcast_to(x, (8, TILE))
    for s in range(TILE // 8):
        r0 = 8 * s
        inside = (lane >= r0) & (lane < r0 + 8)
        rows = [spread(d_ref[r0 + j : r0 + j + 1, :]) for j in range(8)]
        e = [
            [spread(rows[i][:, r0 + j : r0 + j + 1]) if j >= i else None for j in range(8)]
            for i in range(8)
        ]
        below = {}
        for i in range(s + 1, TILE // 8):
            b = d_ref[8 * i : 8 * i + 8, :]
            below[i] = (b, [spread(b[:, r0 + j : r0 + j + 1]) for j in range(8)])
        u = [jnp.where(inside, (lane == r0 + j).astype(f32), rows[j]) for j in range(8)]
        ys, rs = [], []
        for j in range(8):
            y = lax.rsqrt(e[j][j])
            r = y * y
            ys.append(y)
            rs.append(r)
            for i in range(j + 1, 8):
                f = e[j][i] * r
                for q in range(i, 8):
                    e[i][q] = e[i][q] - f * e[j][q]
                u[i] = u[i] - f * u[j]
        out = u[7] * ys[7]
        for j in range(6, -1, -1):
            out = jnp.where(sub == j, u[j] * ys[j], out)
        g = [None] * 8
        for j in range(7, -1, -1):
            acc = u[j] * rs[j]
            for i in range(j + 1, 8):
                acc = acc - (e[j][i] * rs[j]) * g[i]
            g[j] = acc
        d_ref[r0 : r0 + 8, :] = out
        for i in range(s + 1, TILE // 8):
            b, c = below[i]
            acc = jnp.where(inside, 0.0, b)
            for j in range(8):
                acc = acc - c[j] * g[j]
            d_ref[8 * i : 8 * i + 8, :] = acc


def place_points(src_ref, raw_ref, p_ref):
    def place(b, carry):
        pair = [raw_ref[src_ref[2 * b + n]].astype(f32) for n in range(2)]
        at = pl.ds(pl.multiple_of(b * 2 * GROUP, 2 * GROUP), 2 * GROUP)
        p_ref[at, :] = jnp.concatenate(pair, axis=0).astype(bf16)
        return carry

    lax.fori_loop(0, PANEL // (2 * GROUP), place, 0)


def local_kernel(info_ref, x_ref, q_ref, p_ref, out_ref, tab_ref, after):
    for b in range(PANEL // 256):
        out_ref[:, b * 256 : (b + 1) * 256] = nt(x_ref[...], p_ref[b * 256 : (b + 1) * 256, :])
    start = info_ref[0] + after
    place = info_ref[1 + after] * GROUP
    column = lax.broadcasted_iota(jnp.int32, (GROUP, PANEL), 1)
    within = lax.broadcasted_iota(jnp.int32, (GROUP, PANEL), 0)

    def clear(r, carry):
        at = pl.ds(pl.multiple_of(r * GROUP, GROUP), GROUP)
        out_ref[at, :] = jnp.zeros((GROUP, PANEL), f32)
        return carry

    lax.fori_loop(0, start, clear, 0)

    def row_block(r, carry):
        at = pl.ds(pl.multiple_of(r * GROUP, GROUP), GROUP)
        k = relu_layers(out_ref[at, :], q_ref[at, :], tab_ref, 0, PANEL)
        own = (r == start) & (column == place + within)
        out_ref[at, :] = k + jnp.where(own, noise_var, 0.0)
        return carry

    lax.fori_loop(start, out_ref.shape[0] // GROUP, row_block, 0)


def panel_kernel(info_ref, src_ref, x_ref, q_ref, raw_ref, out_ref, a_ref, p_ref, tab_ref, qrow_ref):
    place_points(src_ref, raw_ref, p_ref)
    for b in range(STEPS):
        along, down = own_square(p_ref, b * TILE)
        store_columns(tab_ref, b * TILE, along)
        qrow_ref[b * TILE : (b + 1) * TILE, :] = jnp.broadcast_to(down, (TILE, TILE))
    local_kernel(info_ref, x_ref, q_ref, p_ref, out_ref, tab_ref, 0)
    for b in range(PANEL // 256):
        lo = b * 256
        for c in range(b, PANEL // 256):
            a_ref[lo : lo + 256, c * 256 : (c + 1) * 256] = nt(
                p_ref[lo : lo + 256, :], p_ref[c * 256 : (c + 1) * 256, :]
            )

        def row_block(r, carry, lo=lo):
            at = pl.ds(pl.multiple_of(r * GROUP, GROUP), GROUP)
            width = PANEL - lo
            k = relu_layers(a_ref[at, lo:], qrow_ref[at, :], tab_ref, lo, width)
            column = lax.broadcasted_iota(jnp.int32, (GROUP, width), 1) + lo
            within = lax.broadcasted_iota(jnp.int32, (GROUP, width), 0)
            a_ref[at, lo:] = k + jnp.where(column == r * GROUP + within, noise_var, 0.0)
            return carry

        lax.fori_loop(lo // GROUP, (lo + 256) // GROUP, row_block, 0)


def next_kernel(info_ref, src_ref, x_ref, q_ref, raw_ref, out_ref, p_ref, tab_ref):
    place_points(src_ref, raw_ref, p_ref)
    for b in range(STEPS):
        store_columns(tab_ref, b * TILE, own_square(p_ref, b * TILE)[0])
    local_kernel(info_ref, x_ref, q_ref, p_ref, out_ref, tab_ref, 1)


def factor_kernel(info_ref, k_ref, m_ref, f_ref, a_ref, inv_ref, d_ref):
    a_ref[...] = m_ref[...]
    row = lax.broadcasted_iota(jnp.int32, (TILE, TILE), 0)
    col = lax.broadcasted_iota(jnp.int32, (TILE, TILE), 1)
    f_ref[...] = k_ref[...]

    def step(k, carry):
        k0 = pl.multiple_of(k * TILE, TILE)
        d_ref[...] = a_ref[pl.ds(k0, TILE), pl.ds(k0, TILE)]
        block_inverse(d_ref)
        linv = jnp.where(row >= col, d_ref[...], 0.0)
        inv_ref[k] = linv
        for kk in range(STEPS - 1):

            @pl.when(k == kk)
            def _():
                b0, c0 = kk * TILE, (kk + 1) * TILE
                u = nn(lhs6(linv), rhs6_nn(a_ref[b0:c0, c0:]))
                a_ref[b0:c0, c0:] = u
                u6 = rhs6_nn(u)
                for i in range(kk + 1, STEPS):
                    i0 = i * TILE
                    x = u[:, i0 - c0 : i0 - c0 + TILE].T
                    a_ref[i0 : i0 + TILE, i0:] = a_ref[i0 : i0 + TILE, i0:] - nn(
                        lhs6(x), u6[:, i0 - c0 :]
                    )

        return carry

    lax.fori_loop(0, STEPS, step, 0)

    for k in range(STEPS):
        b0, c0 = k * TILE, (k + 1) * TILE
        x = nt(lhs6(f_ref[:, b0:c0]), rhs6_nt(inv_ref[k]))
        f_ref[:, b0:c0] = x
        if k < STEPS - 1:
            f_ref[:, c0:] = f_ref[:, c0:] - nn(lhs6(x), rhs6_nn(a_ref[b0:c0, c0:]))

    at = pl.ds(pl.multiple_of(info_ref[0] * GROUP, GROUP), GROUP)
    column = lax.broadcasted_iota(jnp.int32, (GROUP, PANEL), 1)
    within = lax.broadcasted_iota(jnp.int32, (GROUP, PANEL), 0)
    f_ref[at, :] = jnp.where(column <= info_ref[1] * GROUP + within, f_ref[at, :], 0.0)


def update_kernel(info_ref, src_ref, f_ref, a_ref, inv_ref, nk_ref, nl_ref, out_ref, g_ref, kn_ref):
    def place(b, carry):
        at = pl.ds(pl.multiple_of(b * GROUP, GROUP), GROUP)
        kn_ref[at, :] = nk_ref[src_ref[b]]
        return carry

    lax.fori_loop(0, PANEL // GROUP, place, 0, unroll=8)
    for k in range(STEPS - 1, -1, -1):
        b0, c0 = k * TILE, (k + 1) * TILE
        x = f_ref[:, b0:c0]
        for j in range(k + 1, STEPS):
            j0 = j * TILE
            x = x - nt(lhs6(g_ref[:, j0 : j0 + TILE]), rhs6_nt(a_ref[b0:c0, j0 : j0 + TILE]))
        g_ref[:, b0:c0] = nn(lhs6(x), rhs6_nn(inv_ref[k]))
    rows = lax.broadcasted_iota(jnp.int32, (f_ref.shape[0], 256), 0) // GROUP
    live = rows > info_ref[0]
    for b in range(PANEL // 256):
        total = nl_ref[:, b * 256 : (b + 1) * 256]
        for k in range(STEPS):
            k0 = k * TILE
            total = total - nt(
                lhs6(g_ref[:, k0 : k0 + TILE]),
                rhs6_nt(kn_ref[b * 256 : (b + 1) * 256, k0 : k0 + TILE]),
            )
        out_ref[:, b * 256 : (b + 1) * 256] = jnp.where(live, total, 0.0)


SMEM = pl.BlockSpec(memory_space=pltpu.SMEM)
VMEM = pl.BlockSpec(memory_space=pltpu.VMEM)
PARAMS = pltpu.CompilerParams(vmem_limit_bytes=56 * 1024 * 1024)


def row_variance(rows):
    values = rows.astype(f32)
    return jnp.sum(values * values, axis=1) * (weight_var / rows.shape[1]) + bias_var


def body(images, block_id, panel_index):
    rows_dev, features = images.shape
    shards = lax.axis_size("row") * lax.axis_size("sub")
    myself = lax.axis_index("row") * lax.axis_size("sub") + lax.axis_index("sub")
    panel = panel_index[0]
    everyone = jnp.arange(shards, dtype=jnp.int32)
    local_var = jnp.broadcast_to(row_variance(images)[:, None], (rows_dev, TILE))

    def arrangement(which):
        positions = lax.dynamic_index_in_dim(block_id, which, 1, keepdims=False) - which * shards
        sources = jnp.sum(
            jnp.where(positions[None, :] == everyone[:, None], everyone[None, :], 0), axis=1
        )
        return sources, positions[myself]

    def gather(block):
        return lax.all_gather(block, ("row", "sub"), axis=0, tiled=True).reshape(
            shards, GROUP, -1
        )

    def own(which, array):
        return lax.dynamic_slice_in_dim(array, which * GROUP, GROUP, 0)

    sources, position = arrangement(panel)
    next_sources, next_position = arrangement(panel + 1)
    info = jnp.stack([panel, position, next_position])
    points = gather(own(panel, images))
    next_points = gather(own(panel + 1, images))
    table = pltpu.VMEM((24, PANEL), f32)
    placed = pltpu.VMEM((PANEL, features), bf16)
    rows_out = jax.ShapeDtypeStruct((rows_dev, PANEL), f32)
    square = jax.ShapeDtypeStruct((PANEL, PANEL), f32)

    matrix, diagonal = pl.pallas_call(
        panel_kernel,
        out_shape=(rows_out, square),
        in_specs=[SMEM, SMEM, VMEM, VMEM, VMEM],
        out_specs=(VMEM, VMEM),
        scratch_shapes=[placed, table, pltpu.VMEM((PANEL, TILE), f32)],
        compiler_params=PARAMS,
        name="panel_kernel",
        cost_estimate=pl.CostEstimate(flops=3 * 10**10, bytes_accessed=16 << 20, transcendentals=0),
    )(info, sources, images, local_var, points)
    next_rows = gather(own(panel + 1, matrix))
    factor, upper, inverses = pl.pallas_call(
        factor_kernel,
        out_shape=(rows_out, square, jax.ShapeDtypeStruct((STEPS, TILE, TILE), f32)),
        in_specs=[SMEM, VMEM, VMEM],
        out_specs=(VMEM, VMEM, VMEM),
        scratch_shapes=[pltpu.VMEM((TILE, TILE), f32)],
        compiler_params=PARAMS,
        name="factor_kernel",
        cost_estimate=pl.CostEstimate(flops=10**11, bytes_accessed=16 << 20, transcendentals=0),
    )(info, matrix, diagonal)
    next_matrix = pl.pallas_call(
        next_kernel,
        out_shape=rows_out,
        in_specs=[SMEM, SMEM, VMEM, VMEM, VMEM],
        out_specs=VMEM,
        scratch_shapes=[placed, table],
        compiler_params=PARAMS,
        name="next_kernel",
        cost_estimate=pl.CostEstimate(flops=2 * 10**10, bytes_accessed=16 << 20, transcendentals=0),
    )(info, next_sources, images, local_var, next_points)
    updated = pl.pallas_call(
        update_kernel,
        out_shape=jax.ShapeDtypeStruct((rows_dev, PANEL), f32),
        in_specs=[SMEM, SMEM, VMEM, VMEM, VMEM, VMEM, VMEM],
        out_specs=VMEM,
        scratch_shapes=[pltpu.VMEM((rows_dev, PANEL), f32), pltpu.VMEM((PANEL, PANEL), f32)],
        compiler_params=PARAMS,
        name="update_kernel",
        cost_estimate=pl.CostEstimate(flops=10**10, bytes_accessed=16 << 20, transcendentals=0),
    )(info, next_sources, factor, upper, inverses, next_rows, next_matrix)
    return (factor, updated)


def solution(mesh):
    in_specs = (P(("row", "sub"), None), P(), P())
    out_specs = (P(("row", "sub"), None), P(("row", "sub"), None))
    return jax.shard_map(body, mesh=mesh, in_specs=in_specs, out_specs=out_specs, check_vma=False)
```

```python
import math

import jax
import jax.numpy as jnp
from jax import lax
from jax.experimental import pallas as pl
from jax.experimental.pallas import tpu as pltpu
from jax.sharding import PartitionSpec as P

PANEL = 1024
DEPTH = 10
GROUP = 8
TILE = 128
STEPS = PANEL // TILE

weight_var = 2.0
bias_var = 0.1
noise_var = 0.1
f32 = jnp.float32
bf16 = jnp.bfloat16

ARC = (
    0.30010470747947693,
    0.015018727630376816,
    0.0023307923693209887,
    0.0007760883891023695,
    -0.00012745900312438607,
    0.00020702359324786812,
)


def nn(a, b):
    return lax.dot_general(a, b, (((1,), (0,)), ((), ())), preferred_element_type=f32)


def nt(a, b):
    return lax.dot_general(a, b, (((1,), (1,)), ((), ())), preferred_element_type=f32)


def split3(x):
    h = x.astype(bf16)
    r = x - h.astype(f32)
    m = r.astype(bf16)
    l = (r - m.astype(f32)).astype(bf16)
    return h, m, l


def lhs6(x):
    h, m, l = split3(x)
    return jnp.concatenate([h, m, h, m, h, l], 1)


def rhs6_nn(x):
    h, m, l = split3(x)
    return jnp.concatenate([h, h, m, m, l, h], 0)


def rhs6_nt(x):
    h, m, l = split3(x)
    return jnp.concatenate([h, h, m, m, l, h], 1)


def own_square(rows_ref, start):
    rows = rows_ref[start : start + TILE, :]
    gram = nt(rows, rows)
    eye = lax.broadcasted_iota(jnp.int32, (TILE, TILE), 0) == lax.broadcasted_iota(
        jnp.int32, (TILE, TILE), 1
    )
    only = jnp.where(eye, gram, 0.0)
    scale = weight_var / rows_ref.shape[1]
    return (
        jnp.sum(only, axis=0, keepdims=True) * scale + bias_var,
        jnp.sum(only, axis=1, keepdims=True) * scale + bias_var,
    )


def layer_scales(q):
    inv = [lax.rsqrt(q + bias_var * n) for n in range(DEPTH)]
    ratio = [(q + bias_var * n) * inv[n] * inv[n + 1] for n in range(DEPTH - 1)]
    offset = [inv[n + 1] * math.sqrt(bias_var) for n in range(DEPTH - 1)]
    last = (q + bias_var * (DEPTH - 1)) * inv[DEPTH - 1]
    return inv[0], ratio, offset, last


def store_columns(tab_ref, start, q):
    first, ratio, offset, last = layer_scales(q)
    for at, row in enumerate([first] + ratio + offset + [last]):
        tab_ref[at : at + 1, start : start + TILE] = row


def relu_layers(gram, q_rows, tab_ref, lo, width):
    first, ratio, offset, last = layer_scales(q_rows)
    pieces = width // TILE
    col = lambda at, w: jnp.broadcast_to(
        tab_ref[at : at + 1, lo + w * TILE : lo + (w + 1) * TILE], (GROUP, TILE)
    )
    scale = weight_var / 3072
    c = [
        (gram[:, w * TILE : (w + 1) * TILE] * scale + bias_var) * (first * col(0, w))
        for w in range(pieces)
    ]
    for n in range(DEPTH):
        for w in range(pieces):
            u = jnp.maximum(1.0 - jnp.abs(c[w]), 1e-30)
            p = ARC[5] * u + ARC[4]
            for k in (3, 2, 1, 0):
                p = p * u + ARC[k]
            g = jnp.maximum(c[w], 0.0) + (u * u) * lax.rsqrt(u) * p
            if n < DEPTH - 1:
                c[w] = g * (ratio[n] * col(1 + n, w)) + offset[n] * col(DEPTH + n, w)
            else:
                c[w] = g * (last * col(2 * DEPTH - 1, w)) + bias_var
    return jnp.concatenate(c, axis=1)


def block_inverse(d_ref):
    lane = lax.broadcasted_iota(jnp.int32, (8, TILE), 1)
    sub = lax.broadcasted_iota(jnp.int32, (8, TILE), 0)
    spread = lambda x: jnp.broadcast_to(x, (8, TILE))
    for s in range(TILE // 8):
        r0 = 8 * s
        inside = (lane >= r0) & (lane < r0 + 8)
        rows = [spread(d_ref[r0 + j : r0 + j + 1, :]) for j in range(8)]
        e = [
            [spread(rows[i][:, r0 + j : r0 + j + 1]) if j >= i else None for j in range(8)]
            for i in range(8)
        ]
        below = {}
        for i in range(s + 1, TILE // 8):
            b = d_ref[8 * i : 8 * i + 8, :]
            below[i] = (b, [spread(b[:, r0 + j : r0 + j + 1]) for j in range(8)])
        u = [jnp.where(inside, (lane == r0 + j).astype(f32), rows[j]) for j in range(8)]
        ys, rs = [], []
        for j in range(8):
            y = lax.rsqrt(e[j][j])
            r = y * y
            ys.append(y)
            rs.append(r)
            for i in range(j + 1, 8):
                f = e[j][i] * r
                for q in range(i, 8):
                    e[i][q] = e[i][q] - f * e[j][q]
                u[i] = u[i] - f * u[j]
        out = u[7] * ys[7]
        for j in range(6, -1, -1):
            out = jnp.where(sub == j, u[j] * ys[j], out)
        g = [None] * 8
        for j in range(7, -1, -1):
            acc = u[j] * rs[j]
            for i in range(j + 1, 8):
                acc = acc - (e[j][i] * rs[j]) * g[i]
            g[j] = acc
        d_ref[r0 : r0 + 8, :] = out
        for i in range(s + 1, TILE // 8):
            b, c = below[i]
            acc = jnp.where(inside, 0.0, b)
            for j in range(8):
                acc = acc - c[j] * g[j]
            d_ref[8 * i : 8 * i + 8, :] = acc


def place_points(src_ref, raw_ref, p_ref):
    def place(b, carry):
        pair = [raw_ref[src_ref[2 * b + n]].astype(f32) for n in range(2)]
        at = pl.ds(pl.multiple_of(b * 2 * GROUP, 2 * GROUP), 2 * GROUP)
        p_ref[at, :] = jnp.concatenate(pair, axis=0).astype(bf16)
        return carry

    lax.fori_loop(0, PANEL // (2 * GROUP), place, 0)


def local_kernel(info_ref, x_ref, q_ref, p_ref, out_ref, tab_ref, after):
    for b in range(PANEL // 256):
        out_ref[:, b * 256 : (b + 1) * 256] = nt(x_ref[...], p_ref[b * 256 : (b + 1) * 256, :])
    start = info_ref[0] + after
    place = info_ref[1 + after] * GROUP
    column = lax.broadcasted_iota(jnp.int32, (GROUP, PANEL), 1)
    within = lax.broadcasted_iota(jnp.int32, (GROUP, PANEL), 0)

    def clear(r, carry):
        at = pl.ds(pl.multiple_of(r * GROUP, GROUP), GROUP)
        out_ref[at, :] = jnp.zeros((GROUP, PANEL), f32)
        return carry

    lax.fori_loop(0, start, clear, 0)

    def row_block(r, carry):
        at = pl.ds(pl.multiple_of(r * GROUP, GROUP), GROUP)
        k = relu_layers(out_ref[at, :], q_ref[at, :], tab_ref, 0, PANEL)
        own = (r == start) & (column == place + within)
        out_ref[at, :] = k + jnp.where(own, noise_var, 0.0)
        return carry

    lax.fori_loop(start, out_ref.shape[0] // GROUP, row_block, 0)


def panel_kernel(info_ref, src_ref, x_ref, q_ref, raw_ref, out_ref, a_ref, p_ref, tab_ref, qrow_ref):
    place_points(src_ref, raw_ref, p_ref)
    for b in range(STEPS):
        along, down = own_square(p_ref, b * TILE)
        store_columns(tab_ref, b * TILE, along)
        qrow_ref[b * TILE : (b + 1) * TILE, :] = jnp.broadcast_to(down, (TILE, TILE))
    local_kernel(info_ref, x_ref, q_ref, p_ref, out_ref, tab_ref, 0)
    for b in range(PANEL // 256):
        lo = b * 256
        for c in range(b, PANEL // 256):
            a_ref[lo : lo + 256, c * 256 : (c + 1) * 256] = nt(
                p_ref[lo : lo + 256, :], p_ref[c * 256 : (c + 1) * 256, :]
            )

        def row_block(r, carry, lo=lo):
            at = pl.ds(pl.multiple_of(r * GROUP, GROUP), GROUP)
            width = PANEL - lo
            k = relu_layers(a_ref[at, lo:], qrow_ref[at, :], tab_ref, lo, width)
            column = lax.broadcasted_iota(jnp.int32, (GROUP, width), 1) + lo
            within = lax.broadcasted_iota(jnp.int32, (GROUP, width), 0)
            a_ref[at, lo:] = k + jnp.where(column == r * GROUP + within, noise_var, 0.0)
            return carry

        lax.fori_loop(lo // GROUP, (lo + 256) // GROUP, row_block, 0)


def next_kernel(info_ref, src_ref, x_ref, q_ref, raw_ref, out_ref, p_ref, tab_ref):
    place_points(src_ref, raw_ref, p_ref)
    for b in range(STEPS):
        store_columns(tab_ref, b * TILE, own_square(p_ref, b * TILE)[0])
    local_kernel(info_ref, x_ref, q_ref, p_ref, out_ref, tab_ref, 1)


def factor_kernel(info_ref, k_ref, m_ref, f_ref, a_ref, inv_ref, d_ref):
    a_ref[...] = m_ref[...]
    row = lax.broadcasted_iota(jnp.int32, (TILE, TILE), 0)
    col = lax.broadcasted_iota(jnp.int32, (TILE, TILE), 1)
    f_ref[...] = k_ref[...]

    def step(k, carry):
        k0 = pl.multiple_of(k * TILE, TILE)
        d_ref[...] = a_ref[pl.ds(k0, TILE), pl.ds(k0, TILE)]
        block_inverse(d_ref)
        linv = jnp.where(row >= col, d_ref[...], 0.0)
        inv_ref[k] = linv
        for kk in range(STEPS - 1):

            @pl.when(k == kk)
            def _():
                b0, c0 = kk * TILE, (kk + 1) * TILE
                u = nn(lhs6(linv), rhs6_nn(a_ref[b0:c0, c0:]))
                a_ref[b0:c0, c0:] = u
                u6 = rhs6_nn(u)
                for i in range(kk + 1, STEPS):
                    i0 = i * TILE
                    x = u[:, i0 - c0 : i0 - c0 + TILE].T
                    a_ref[i0 : i0 + TILE, i0:] = a_ref[i0 : i0 + TILE, i0:] - nn(
                        lhs6(x), u6[:, i0 - c0 :]
                    )

        return carry

    lax.fori_loop(0, STEPS, step, 0)

    for k in range(STEPS):
        b0, c0 = k * TILE, (k + 1) * TILE
        x = nt(lhs6(f_ref[:, b0:c0]), rhs6_nt(inv_ref[k]))
        f_ref[:, b0:c0] = x
        if k < STEPS - 1:
            f_ref[:, c0:] = f_ref[:, c0:] - nn(lhs6(x), rhs6_nn(a_ref[b0:c0, c0:]))

    at = pl.ds(pl.multiple_of(info_ref[0] * GROUP, GROUP), GROUP)
    column = lax.broadcasted_iota(jnp.int32, (GROUP, PANEL), 1)
    within = lax.broadcasted_iota(jnp.int32, (GROUP, PANEL), 0)
    f_ref[at, :] = jnp.where(column <= info_ref[1] * GROUP + within, f_ref[at, :], 0.0)


def update_kernel(info_ref, src_ref, f_ref, a_ref, inv_ref, nk_ref, nl_ref, out_ref, g_ref, kn_ref):
    def place(b, carry):
        at = pl.ds(pl.multiple_of(b * GROUP, GROUP), GROUP)
        kn_ref[at, :] = nk_ref[src_ref[b]]
        return carry

    lax.fori_loop(0, PANEL // GROUP, place, 0, unroll=8)
    for k in range(STEPS - 1, -1, -1):
        b0, c0 = k * TILE, (k + 1) * TILE
        x = f_ref[:, b0:c0]
        for j in range(k + 1, STEPS):
            j0 = j * TILE
            x = x - nt(lhs6(g_ref[:, j0 : j0 + TILE]), rhs6_nt(a_ref[b0:c0, j0 : j0 + TILE]))
        g_ref[:, b0:c0] = nn(lhs6(x), rhs6_nn(inv_ref[k]))
    rows = lax.broadcasted_iota(jnp.int32, (f_ref.shape[0], 256), 0) // GROUP
    live = rows > info_ref[0]
    for b in range(PANEL // 256):
        total = nl_ref[:, b * 256 : (b + 1) * 256]
        for k in range(STEPS):
            k0 = k * TILE
            total = total - nt(
                lhs6(g_ref[:, k0 : k0 + TILE]),
                rhs6_nt(kn_ref[b * 256 : (b + 1) * 256, k0 : k0 + TILE]),
            )
        out_ref[:, b * 256 : (b + 1) * 256] = jnp.where(live, total, 0.0)


ORDERS = (("x", "y", "z"), ("y", "z", "x"), ("z", "x", "y"))


def gather_kernel(block_ref, out_ref, near_send, near_recv, pair_send, pair_recv, own_sem, *, cuts):
    row, sub = lax.axis_index("row"), lax.axis_index("sub")
    me = {"z": row // 8, "y": row // 2 % 4, "x": sub}
    core = row % 2

    def device(at, core_at):
        return (at["z"] * 8 + at["y"] * 2 + core_at, at["x"])

    def shifted(axis, by):
        return {**me, axis: (me[axis] + by + 4) % 4}

    partner = device(me, 1 - core)
    peers = [device(shifted(a, by), core) for a in "zyx" for by in (1, -1)] + [partner]
    barrier = pltpu.get_barrier_semaphore()
    for peer in peers:
        pl.semaphore_signal(barrier, inc=1, device_id=peer, device_id_type=pl.DeviceIdType.MESH)
    pl.semaphore_wait(barrier, len(peers))

    def part(at, core_at, lo, hi):
        return out_ref.at[at["z"], at["y"], core_at, at["x"], :, lo:hi]

    def copy(src, dst, send, recv, to):
        return pltpu.make_async_remote_copy(
            src_ref=src,
            dst_ref=dst,
            send_sem=send,
            recv_sem=recv,
            device_id=to,
            device_id_type=pl.DeviceIdType.MESH,
        )

    every = pl.ds(0, 4)
    width = block_ref.shape[1]
    mine = pltpu.make_async_copy(block_ref, part(me, core, 0, width), own_sem)
    mine.start()
    sent = []

    def to_partner(at, lo, hi, slot):
        c = copy(part(at, core, lo, hi), part(at, core, lo, hi), pair_send.at[slot], pair_recv.at[slot], partner)
        c.start()
        arriving.append(
            copy(part(at, 1 - core, lo, hi), part(at, 1 - core, lo, hi), pair_send.at[slot], pair_recv.at[slot], partner)
        )
        sent.append(c)

    arriving = []
    for t in range(3):
        held = []
        for s, order in enumerate(ORDERS):
            lo, mid, hi = cuts[s]
            axis = order[t]
            sets = {
                by: {**{a: every if order.index(a) < t else me[a] for a in "zyx"}, axis: (me[axis] + by + 4) % 4}
                for by in (0, 1, -1, 2)
            }
            up, down = device(shifted(axis, 1), core), device(shifted(axis, -1), core)

            def near(kind, by, a, b, to, s=s, t=t, sets=sets):
                piece = part(sets[by], core, a, b)
                source = block_ref.at[:, a:b] if t == 0 and by == 0 else piece
                return copy(source, piece, near_send.at[s, t, kind], near_recv.at[s, t, kind], to)

            for kind, to in ((0, up), (1, down)):
                c = near(kind, 0, lo, hi, to)
                c.start()
                sent.append(c)
            held.append((near, sets, up, down, lo, mid, hi))
        if t == 0:
            mine.wait()
            to_partner(me, 0, width, 27)
        for s, (near, sets, up, down, lo, mid, hi) in enumerate(held):
            near(0, -1, lo, hi, up).wait_recv()
            c = near(2, -1, lo, mid, up)
            c.start()
            sent.append(c)
            near(1, 1, lo, hi, down).wait_recv()
            c = near(3, 1, mid, hi, down)
            c.start()
            sent.append(c)
            to_partner(sets[-1], lo, hi, 9 * s + 3 * t)
            to_partner(sets[1], lo, hi, 9 * s + 3 * t + 1)
        for s, (near, sets, up, down, lo, mid, hi) in enumerate(held):
            near(2, 2, lo, mid, up).wait_recv()
            near(3, 2, mid, hi, down).wait_recv()
            to_partner(sets[2], lo, hi, 9 * s + 3 * t + 2)
    for c in arriving:
        c.wait_recv()
    for c in sent:
        c.wait_send()


def gather_blocks(block, collective_id):
    rows, width = block.shape
    tiles = width // 128
    first = [0, tiles * 3 // 8 if tiles % 3 else tiles // 3, tiles * 3 // 4 if tiles % 3 else 2 * tiles // 3, tiles]
    cuts = [(128 * a, 128 * ((a + b + 1) // 2), 128 * b) for a, b in zip(first, first[1:])]
    out = pl.pallas_call(
        lambda *refs: gather_kernel(*refs, cuts=cuts),
        out_shape=jax.ShapeDtypeStruct((4, 4, 2, 4, rows, width), block.dtype),
        in_specs=[pl.BlockSpec(memory_space=pl.ANY)],
        out_specs=pl.BlockSpec(memory_space=pl.ANY),
        scratch_shapes=[
            pltpu.SemaphoreType.DMA((3, 3, 4)),
            pltpu.SemaphoreType.DMA((3, 3, 4)),
            pltpu.SemaphoreType.DMA((28,)),
            pltpu.SemaphoreType.DMA((28,)),
            pltpu.SemaphoreType.DMA,
        ],
        compiler_params=pltpu.CompilerParams(collective_id=collective_id, has_side_effects=True),
        name="gather_kernel",
    )(block)
    return out.reshape(128, rows, width)


SMEM = pl.BlockSpec(memory_space=pltpu.SMEM)
VMEM = pl.BlockSpec(memory_space=pltpu.VMEM)
PARAMS = pltpu.CompilerParams(vmem_limit_bytes=56 * 1024 * 1024)


def row_variance(rows):
    values = rows.astype(f32)
    return jnp.sum(values * values, axis=1) * (weight_var / rows.shape[1]) + bias_var


def body(images, block_id, panel_index):
    rows_dev, features = images.shape
    shards = lax.axis_size("row") * lax.axis_size("sub")
    myself = lax.axis_index("row") * lax.axis_size("sub") + lax.axis_index("sub")
    panel = panel_index[0]
    everyone = jnp.arange(shards, dtype=jnp.int32)
    local_var = jnp.broadcast_to(row_variance(images)[:, None], (rows_dev, TILE))

    def arrangement(which):
        positions = lax.dynamic_index_in_dim(block_id, which, 1, keepdims=False) - which * shards
        sources = jnp.sum(
            jnp.where(positions[None, :] == everyone[:, None], everyone[None, :], 0), axis=1
        )
        return sources, positions[myself]

    def gather(block):
        return lax.all_gather(block, ("row", "sub"), axis=0, tiled=True).reshape(
            shards, GROUP, -1
        )

    def own(which, array):
        return lax.dynamic_slice_in_dim(array, which * GROUP, GROUP, 0)

    sources, position = arrangement(panel)
    next_sources, next_position = arrangement(panel + 1)
    info = jnp.stack([panel, position, next_position])
    points = gather_blocks(own(panel, images), 0)
    next_points = gather(own(panel + 1, images))
    table = pltpu.VMEM((24, PANEL), f32)
    placed = pltpu.VMEM((PANEL, features), bf16)
    rows_out = jax.ShapeDtypeStruct((rows_dev, PANEL), f32)
    square = jax.ShapeDtypeStruct((PANEL, PANEL), f32)

    matrix, diagonal = pl.pallas_call(
        panel_kernel,
        out_shape=(rows_out, square),
        in_specs=[SMEM, SMEM, VMEM, VMEM, VMEM],
        out_specs=(VMEM, VMEM),
        scratch_shapes=[placed, table, pltpu.VMEM((PANEL, TILE), f32)],
        compiler_params=PARAMS,
        name="panel_kernel",
        cost_estimate=pl.CostEstimate(flops=3 * 10**10, bytes_accessed=16 << 20, transcendentals=0),
    )(info, sources, images, local_var, points)
    next_rows = gather(own(panel + 1, matrix))
    factor, upper, inverses = pl.pallas_call(
        factor_kernel,
        out_shape=(rows_out, square, jax.ShapeDtypeStruct((STEPS, TILE, TILE), f32)),
        in_specs=[SMEM, VMEM, VMEM],
        out_specs=(VMEM, VMEM, VMEM),
        scratch_shapes=[pltpu.VMEM((TILE, TILE), f32)],
        compiler_params=PARAMS,
        name="factor_kernel",
        cost_estimate=pl.CostEstimate(flops=10**11, bytes_accessed=16 << 20, transcendentals=0),
    )(info, matrix, diagonal)
    next_matrix = pl.pallas_call(
        next_kernel,
        out_shape=rows_out,
        in_specs=[SMEM, SMEM, VMEM, VMEM, VMEM],
        out_specs=VMEM,
        scratch_shapes=[placed, table],
        compiler_params=PARAMS,
        name="next_kernel",
        cost_estimate=pl.CostEstimate(flops=2 * 10**10, bytes_accessed=16 << 20, transcendentals=0),
    )(info, next_sources, images, local_var, next_points)
    updated = pl.pallas_call(
        update_kernel,
        out_shape=jax.ShapeDtypeStruct((rows_dev, PANEL), f32),
        in_specs=[SMEM, SMEM, VMEM, VMEM, VMEM, VMEM, VMEM],
        out_specs=VMEM,
        scratch_shapes=[pltpu.VMEM((rows_dev, PANEL), f32), pltpu.VMEM((PANEL, PANEL), f32)],
        compiler_params=PARAMS,
        name="update_kernel",
        cost_estimate=pl.CostEstimate(flops=10**10, bytes_accessed=16 << 20, transcendentals=0),
    )(info, next_sources, factor, upper, inverses, next_rows, next_matrix)
    return (factor, updated)


def solution(mesh):
    in_specs = (P(("row", "sub"), None), P(), P())
    out_specs = (P(("row", "sub"), None), P(("row", "sub"), None))
    return jax.shard_map(body, mesh=mesh, in_specs=in_specs, out_specs=out_specs, check_vma=False)
```

```python
import math

import jax
import jax.numpy as jnp
from jax import lax
from jax.experimental import pallas as pl
from jax.experimental.pallas import tpu as pltpu
from jax.sharding import PartitionSpec as P

PANEL = 1024
DEPTH = 10
GROUP = 8
TILE = 128
STEPS = PANEL // TILE

weight_var = 2.0
bias_var = 0.1
noise_var = 0.1
f32 = jnp.float32
bf16 = jnp.bfloat16

ARC_A = 0.2353731889436501
ARC_B = 0.116208962721599
ARC_C = 3.2233309496295237
ARC_D = 0.005000674198862276


def nn(a, b):
    return lax.dot_general(a, b, (((1,), (0,)), ((), ())), preferred_element_type=f32)


def nt(a, b):
    return lax.dot_general(a, b, (((1,), (1,)), ((), ())), preferred_element_type=f32)


def split3(x):
    h = x.astype(bf16)
    r = x - h.astype(f32)
    m = r.astype(bf16)
    l = (r - m.astype(f32)).astype(bf16)
    return h, m, l


def lhs6(x):
    h, m, l = split3(x)
    return jnp.concatenate([h, m, h, m, h, l], 1)


def rhs6_nn(x):
    h, m, l = split3(x)
    return jnp.concatenate([h, h, m, m, l, h], 0)


def rhs6_nt(x):
    h, m, l = split3(x)
    return jnp.concatenate([h, h, m, m, l, h], 1)


def own_square(rows_ref, start):
    rows = rows_ref[start : start + TILE, :]
    gram = nt(rows, rows)
    eye = lax.broadcasted_iota(jnp.int32, (TILE, TILE), 0) == lax.broadcasted_iota(
        jnp.int32, (TILE, TILE), 1
    )
    only = jnp.where(eye, gram, 0.0)
    scale = weight_var / rows_ref.shape[1]
    return (
        jnp.sum(only, axis=0, keepdims=True) * scale + bias_var,
        jnp.sum(only, axis=1, keepdims=True) * scale + bias_var,
    )


def layer_scales(q):
    inv = [lax.rsqrt(q + bias_var * n) for n in range(DEPTH)]
    ratio = [(q + bias_var * n) * inv[n] * inv[n + 1] for n in range(DEPTH - 1)]
    offset = [inv[n + 1] * math.sqrt(bias_var) for n in range(DEPTH - 1)]
    last = (q + bias_var * (DEPTH - 1)) * inv[DEPTH - 1]
    return inv[0], ratio, offset, last


def store_columns(tab_ref, start, q):
    first, ratio, offset, last = layer_scales(q)
    for at, row in enumerate([first] + ratio + offset + [last]):
        tab_ref[at : at + 1, start : start + TILE] = row


def relu_layers(gram, q_rows, tab_ref, lo, width):
    first, ratio, offset, last = layer_scales(q_rows)
    pieces = width // TILE
    col = lambda at, w: jnp.broadcast_to(
        tab_ref[at : at + 1, lo + w * TILE : lo + (w + 1) * TILE], (GROUP, TILE)
    )
    scale = weight_var / 3072
    c = [
        (gram[:, w * TILE : (w + 1) * TILE] * scale + bias_var) * (first * col(0, w))
        for w in range(pieces)
    ]
    for n in range(DEPTH):
        for w in range(pieces):
            size = jnp.abs(c[w]) if n == 0 else c[w]
            u = jnp.maximum(1.0 - size, 1e-30)
            p = (ARC_D * u + ARC_A) + ARC_B * lax.rsqrt(ARC_C - u)
            g = (jnp.maximum(c[w], 0.0) if n == 0 else c[w]) + (u * u) * lax.rsqrt(u) * p
            if n < DEPTH - 1:
                c[w] = g * (ratio[n] * col(1 + n, w)) + offset[n] * col(DEPTH + n, w)
            else:
                c[w] = g * (last * col(2 * DEPTH - 1, w)) + bias_var
    return jnp.concatenate(c, axis=1)


def total(xs):
    xs = list(xs)
    while len(xs) > 1:
        xs = [xs[i] + xs[i + 1] if i + 1 < len(xs) else xs[i] for i in range(0, len(xs), 2)]
    return xs[0]


def block_inverse(d_ref, cs_ref):
    lane = lax.broadcasted_iota(jnp.int32, (8, TILE), 1)
    sub = lax.broadcasted_iota(jnp.int32, (8, TILE), 0)
    spread = lambda x: jnp.broadcast_to(x, (8, TILE))
    now = d_ref[0:8, :]
    for s in range(TILE // 8):
        r0 = 8 * s
        slot = 64 * (s % 2)
        inside = (lane >= r0) & (lane < r0 + 8)
        for j in range(8):
            cs_ref[slot + 8 * j : slot + 8 * j + 8, :] = spread(now[:, r0 + j : r0 + j + 1])
        e = [
            [
                spread(cs_ref[slot + 8 * j + i : slot + 8 * j + i + 1, :]) if j >= i else None
                for j in range(8)
            ]
            for i in range(8)
        ]
        below = {}
        for i in range(s + 1, TILE // 8):
            b = d_ref[8 * i : 8 * i + 8, :]
            below[i] = (b, [spread(b[:, r0 + j : r0 + j + 1]) for j in range(8)])
        t = [
            jnp.where(inside, (lane == r0 + j).astype(f32), spread(d_ref[r0 + j : r0 + j + 1, :]))
            for j in range(8)
        ]
        w = [[None] * 8 for _ in range(8)]
        z = [None] * 8
        rows = [None] * 8
        for j in range(0, 8, 2):
            a, b, c = e[j][j], e[j][j + 1], e[j + 1][j + 1]
            root_det = lax.rsqrt(a * c - b * b)
            root_a = lax.rsqrt(a)
            rd = root_det * root_det
            for i in range(j + 2, 8):
                f0 = (c * e[j][i] - b * e[j + 1][i]) * rd
                f1 = (a * e[j + 1][i] - b * e[j][i]) * rd
                for q in range(i, 8):
                    e[i][q] = e[i][q] - (f0 * e[j][q] + f1 * e[j + 1][q])
                t[i] = t[i] - (f0 * t[j] + f1 * t[j + 1])
                for k in range(j):
                    w[i][k] = w[i][k] - (f0 * w[j][k] + f1 * w[j + 1][k])
                w[i][j], w[i][j + 1] = -f0, -f1
            z[j] = (c * t[j] - b * t[j + 1]) * rd
            z[j + 1] = (a * t[j + 1] - b * t[j]) * rd
            rows[j] = t[j] * root_a
            rows[j + 1] = (t[j + 1] - (b * (root_a * root_a)) * t[j]) * (root_det * (a * root_a))
        g = [total([z[k]] + [w[i][k] * z[i] for i in range(k // 2 * 2 + 2, 8)]) for k in range(8)]
        out = rows[7]
        for j in range(6, -1, -1):
            out = jnp.where(sub == j, rows[j], out)
        d_ref[r0 : r0 + 8, :] = out
        for i in range(s + 1, TILE // 8):
            b, c = below[i]
            acc = jnp.where(inside, 0.0, b) - total([c[j] * g[j] for j in range(8)])
            d_ref[8 * i : 8 * i + 8, :] = acc
            if i == s + 1:
                now = acc


def place_points(src_ref, raw_ref, p_ref):
    def place(b, carry):
        pair = [raw_ref[src_ref[2 * b + n]].astype(f32) for n in range(2)]
        at = pl.ds(pl.multiple_of(b * 2 * GROUP, 2 * GROUP), 2 * GROUP)
        p_ref[at, :] = jnp.concatenate(pair, axis=0).astype(bf16)
        return carry

    lax.fori_loop(0, PANEL // (2 * GROUP), place, 0)


def local_kernel(info_ref, x_ref, q_ref, p_ref, out_ref, tab_ref, after):
    for b in range(PANEL // 256):
        out_ref[:, b * 256 : (b + 1) * 256] = nt(x_ref[...], p_ref[b * 256 : (b + 1) * 256, :])
    start = info_ref[0] + after
    place = info_ref[1 + after] * GROUP
    column = lax.broadcasted_iota(jnp.int32, (GROUP, PANEL), 1)
    within = lax.broadcasted_iota(jnp.int32, (GROUP, PANEL), 0)

    def clear(r, carry):
        at = pl.ds(pl.multiple_of(r * GROUP, GROUP), GROUP)
        out_ref[at, :] = jnp.zeros((GROUP, PANEL), f32)
        return carry

    lax.fori_loop(0, start, clear, 0)

    def row_block(r, carry):
        at = pl.ds(pl.multiple_of(r * GROUP, GROUP), GROUP)
        k = relu_layers(out_ref[at, :], q_ref[at, :], tab_ref, 0, PANEL)
        own = (r == start) & (column == place + within)
        out_ref[at, :] = k + jnp.where(own, noise_var, 0.0)
        return carry

    lax.fori_loop(start, out_ref.shape[0] // GROUP, row_block, 0)


def cross_kernel(info_ref, src_ref, x_ref, q_ref, raw_ref, out_ref, p_ref, tab_ref, *, after):
    place_points(src_ref, raw_ref, p_ref)
    for b in range(STEPS):
        store_columns(tab_ref, b * TILE, own_square(p_ref, b * TILE)[0])
    local_kernel(info_ref, x_ref, q_ref, p_ref, out_ref, tab_ref, after)


def factor_kernel(
    info_ref, src_ref, raw_ref, k_ref, f_ref, g_ref, p_ref, a_ref, inv_ref, tab_ref, qrow_ref, d_ref, cs_ref
):
    place_points(src_ref, raw_ref, p_ref)
    for b in range(STEPS):
        along, down = own_square(p_ref, b * TILE)
        store_columns(tab_ref, b * TILE, along)
        qrow_ref[b * TILE : (b + 1) * TILE, :] = jnp.broadcast_to(down, (TILE, TILE))
    for b in range(PANEL // 256):
        lo = b * 256
        for c in range(b, PANEL // 256):
            a_ref[lo : lo + 256, c * 256 : (c + 1) * 256] = nt(
                p_ref[lo : lo + 256, :], p_ref[c * 256 : (c + 1) * 256, :]
            )

        def row_block(r, carry, lo=lo):
            at = pl.ds(pl.multiple_of(r * GROUP, GROUP), GROUP)
            width = PANEL - lo
            k = relu_layers(a_ref[at, lo:], qrow_ref[at, :], tab_ref, lo, width)
            column = lax.broadcasted_iota(jnp.int32, (GROUP, width), 1) + lo
            within = lax.broadcasted_iota(jnp.int32, (GROUP, width), 0)
            a_ref[at, lo:] = k + jnp.where(column == r * GROUP + within, noise_var, 0.0)
            return carry

        lax.fori_loop(lo // GROUP, (lo + 256) // GROUP, row_block, 0)

    row = lax.broadcasted_iota(jnp.int32, (TILE, TILE), 0)
    col = lax.broadcasted_iota(jnp.int32, (TILE, TILE), 1)
    f_ref[...] = k_ref[...]

    def step(k, carry):
        k0 = pl.multiple_of(k * TILE, TILE)
        d_ref[...] = a_ref[pl.ds(k0, TILE), pl.ds(k0, TILE)]
        block_inverse(d_ref, cs_ref)
        linv = jnp.where(row >= col, d_ref[...], 0.0)
        inv_ref[k] = linv
        for kk in range(STEPS - 1):

            @pl.when(k == kk)
            def _():
                b0, c0 = kk * TILE, (kk + 1) * TILE
                u = nn(lhs6(linv), rhs6_nn(a_ref[b0:c0, c0:]))
                a_ref[b0:c0, c0:] = u
                u6 = rhs6_nn(u)
                for i in range(kk + 1, STEPS):
                    i0 = i * TILE
                    x = u[:, i0 - c0 : i0 - c0 + TILE].T
                    a_ref[i0 : i0 + TILE, i0:] = a_ref[i0 : i0 + TILE, i0:] - nn(
                        lhs6(x), u6[:, i0 - c0 :]
                    )

        return carry

    lax.fori_loop(0, STEPS, step, 0)

    for k in range(STEPS):
        b0, c0 = k * TILE, (k + 1) * TILE
        x = nt(lhs6(f_ref[:, b0:c0]), rhs6_nt(inv_ref[k]))
        f_ref[:, b0:c0] = x
        if k < STEPS - 1:
            f_ref[:, c0:] = f_ref[:, c0:] - nn(lhs6(x), rhs6_nn(a_ref[b0:c0, c0:]))

    at = pl.ds(pl.multiple_of(info_ref[0] * GROUP, GROUP), GROUP)
    column = lax.broadcasted_iota(jnp.int32, (GROUP, PANEL), 1)
    within = lax.broadcasted_iota(jnp.int32, (GROUP, PANEL), 0)
    f_ref[at, :] = jnp.where(column <= info_ref[1] * GROUP + within, f_ref[at, :], 0.0)

    for k in range(STEPS - 1, -1, -1):
        b0, c0 = k * TILE, (k + 1) * TILE
        x = f_ref[:, b0:c0]
        for j in range(k + 1, STEPS):
            j0 = j * TILE
            x = x - nt(lhs6(g_ref[:, j0 : j0 + TILE]), rhs6_nt(a_ref[b0:c0, j0 : j0 + TILE]))
        g_ref[:, b0:c0] = nn(lhs6(x), rhs6_nn(inv_ref[k]))


def update_kernel(info_ref, src_ref, g_ref, nk_ref, nl_ref, out_ref, kn_ref):
    def place(b, carry):
        at = pl.ds(pl.multiple_of(b * GROUP, GROUP), GROUP)
        kn_ref[at, :] = nk_ref[src_ref[b]]
        return carry

    lax.fori_loop(0, PANEL // GROUP, place, 0, unroll=8)
    rows = lax.broadcasted_iota(jnp.int32, (g_ref.shape[0], 256), 0) // GROUP
    live = rows > info_ref[0]
    for b in range(PANEL // 256):
        total = nl_ref[:, b * 256 : (b + 1) * 256]
        for k in range(STEPS):
            k0 = k * TILE
            total = total - nt(
                lhs6(g_ref[:, k0 : k0 + TILE]),
                rhs6_nt(kn_ref[b * 256 : (b + 1) * 256, k0 : k0 + TILE]),
            )
        out_ref[:, b * 256 : (b + 1) * 256] = jnp.where(live, total, 0.0)


ORDERS = (("x", "y", "z"), ("y", "z", "x"), ("z", "x", "y"))


def gather_kernel(block_ref, out_ref, near_send, near_recv, pair_send, pair_recv, own_sem, *, cuts):
    row, sub = lax.axis_index("row"), lax.axis_index("sub")
    me = {"z": row // 8, "y": row // 2 % 4, "x": sub}
    core = row % 2

    def device(at, core_at):
        return (at["z"] * 8 + at["y"] * 2 + core_at, at["x"])

    def shifted(axis, by):
        return {**me, axis: (me[axis] + by + 4) % 4}

    partner = device(me, 1 - core)
    peers = [device(shifted(a, by), core) for a in "zyx" for by in (1, -1)] + [partner]
    barrier = pltpu.get_barrier_semaphore()
    for peer in peers:
        pl.semaphore_signal(barrier, inc=1, device_id=peer, device_id_type=pl.DeviceIdType.MESH)
    pl.semaphore_wait(barrier, len(peers))

    def part(at, core_at, lo, hi):
        return out_ref.at[at["z"], at["y"], core_at, at["x"], :, lo:hi]

    def copy(src, dst, send, recv, to):
        return pltpu.make_async_remote_copy(
            src_ref=src,
            dst_ref=dst,
            send_sem=send,
            recv_sem=recv,
            device_id=to,
            device_id_type=pl.DeviceIdType.MESH,
        )

    every = pl.ds(0, 4)
    width = block_ref.shape[1]
    mine = pltpu.make_async_copy(block_ref, part(me, core, 0, width), own_sem)
    mine.start()
    sent = []

    def to_partner(at, lo, hi, slot):
        c = copy(part(at, core, lo, hi), part(at, core, lo, hi), pair_send.at[slot], pair_recv.at[slot], partner)
        c.start()
        arriving.append(
            copy(part(at, 1 - core, lo, hi), part(at, 1 - core, lo, hi), pair_send.at[slot], pair_recv.at[slot], partner)
        )
        sent.append(c)

    arriving = []
    for t in range(3):
        held = []
        for s, order in enumerate(ORDERS):
            lo, mid, hi = cuts[s]
            axis = order[t]
            sets = {
                by: {**{a: every if order.index(a) < t else me[a] for a in "zyx"}, axis: (me[axis] + by + 4) % 4}
                for by in (0, 1, -1, 2)
            }
            up, down = device(shifted(axis, 1), core), device(shifted(axis, -1), core)

            def near(kind, by, a, b, to, s=s, t=t, sets=sets):
                piece = part(sets[by], core, a, b)
                source = block_ref.at[:, a:b] if t == 0 and by == 0 else piece
                return copy(source, piece, near_send.at[s, t, kind], near_recv.at[s, t, kind], to)

            for kind, to in ((0, up), (1, down)):
                c = near(kind, 0, lo, hi, to)
                c.start()
                sent.append(c)
            held.append((near, sets, up, down, lo, mid, hi))
        if t == 0:
            mine.wait()
            to_partner(me, 0, width, 27)
        for s, (near, sets, up, down, lo, mid, hi) in enumerate(held):
            near(0, -1, lo, hi, up).wait_recv()
            c = near(2, -1, lo, mid, up)
            c.start()
            sent.append(c)
            near(1, 1, lo, hi, down).wait_recv()
            c = near(3, 1, mid, hi, down)
            c.start()
            sent.append(c)
            to_partner(sets[-1], lo, hi, 9 * s + 3 * t)
            to_partner(sets[1], lo, hi, 9 * s + 3 * t + 1)
        for s, (near, sets, up, down, lo, mid, hi) in enumerate(held):
            near(2, 2, lo, mid, up).wait_recv()
            near(3, 2, mid, hi, down).wait_recv()
            to_partner(sets[2], lo, hi, 9 * s + 3 * t + 2)
    for c in arriving:
        c.wait_recv()
    for c in sent:
        c.wait_send()


def gather_blocks(block, collective_id):
    rows, width = block.shape
    tiles = width // 128
    first = [0, tiles * 3 // 8 if tiles % 3 else tiles // 3, tiles * 3 // 4 if tiles % 3 else 2 * tiles // 3, tiles]
    cuts = [(128 * a, 128 * ((a + b + 1) // 2), 128 * b) for a, b in zip(first, first[1:])]
    out = pl.pallas_call(
        lambda *refs: gather_kernel(*refs, cuts=cuts),
        out_shape=jax.ShapeDtypeStruct((4, 4, 2, 4, rows, width), block.dtype),
        in_specs=[pl.BlockSpec(memory_space=pl.ANY)],
        out_specs=pl.BlockSpec(memory_space=pl.ANY),
        scratch_shapes=[
            pltpu.SemaphoreType.DMA((3, 3, 4)),
            pltpu.SemaphoreType.DMA((3, 3, 4)),
            pltpu.SemaphoreType.DMA((28,)),
            pltpu.SemaphoreType.DMA((28,)),
            pltpu.SemaphoreType.DMA,
        ],
        compiler_params=pltpu.CompilerParams(collective_id=collective_id, has_side_effects=True),
        name="gather_kernel",
    )(block)
    return out.reshape(128, rows, width)


SMEM = pl.BlockSpec(memory_space=pltpu.SMEM)
VMEM = pl.BlockSpec(memory_space=pltpu.VMEM)
PARAMS = pltpu.CompilerParams(vmem_limit_bytes=56 * 1024 * 1024)


def row_variance(rows):
    values = rows.astype(f32)
    return jnp.sum(values * values, axis=1) * (weight_var / rows.shape[1]) + bias_var


def body(images, block_id, panel_index):
    rows_dev, features = images.shape
    shards = lax.axis_size("row") * lax.axis_size("sub")
    myself = lax.axis_index("row") * lax.axis_size("sub") + lax.axis_index("sub")
    panel = panel_index[0]
    everyone = jnp.arange(shards, dtype=jnp.int32)
    local_var = jnp.broadcast_to(row_variance(images)[:, None], (rows_dev, TILE))

    def arrangement(which):
        positions = lax.dynamic_index_in_dim(block_id, which, 1, keepdims=False) - which * shards
        sources = jnp.sum(
            jnp.where(positions[None, :] == everyone[:, None], everyone[None, :], 0), axis=1
        )
        return sources, positions[myself]

    def gather(block):
        return lax.all_gather(block, ("row", "sub"), axis=0, tiled=True).reshape(
            shards, GROUP, -1
        )

    def own(which, array):
        return lax.dynamic_slice_in_dim(array, which * GROUP, GROUP, 0)

    sources, position = arrangement(panel)
    next_sources, next_position = arrangement(panel + 1)
    info = jnp.stack([panel, position, next_position])
    points = gather_blocks(own(panel, images), 0)
    next_points = gather(own(panel + 1, images))
    table = pltpu.VMEM((24, PANEL), f32)
    placed = pltpu.VMEM((PANEL, features), bf16)
    rows_out = jax.ShapeDtypeStruct((rows_dev, PANEL), f32)

    def cross(blocks, order, after):
        return pl.pallas_call(
            lambda *refs: cross_kernel(*refs, after=after),
            out_shape=rows_out,
            in_specs=[SMEM, SMEM, VMEM, VMEM, VMEM],
            out_specs=VMEM,
            scratch_shapes=[placed, table],
            compiler_params=PARAMS,
            name="cross_kernel",
            cost_estimate=pl.CostEstimate(flops=2 * 10**10, bytes_accessed=16 << 20, transcendentals=0),
        )(info, order, images, local_var, blocks)

    matrix = cross(points, sources, 0)
    next_rows = gather(own(panel + 1, matrix))
    factor, weights = pl.pallas_call(
        factor_kernel,
        out_shape=(rows_out, rows_out),
        in_specs=[SMEM, SMEM, VMEM, VMEM],
        out_specs=(VMEM, VMEM),
        scratch_shapes=[
            placed,
            pltpu.VMEM((PANEL, PANEL), f32),
            pltpu.VMEM((STEPS, TILE, TILE), f32),
            table,
            pltpu.VMEM((PANEL, TILE), f32),
            pltpu.VMEM((TILE, TILE), f32),
            pltpu.VMEM((TILE, TILE), f32),
        ],
        compiler_params=PARAMS,
        name="factor_kernel",
        cost_estimate=pl.CostEstimate(flops=10**11, bytes_accessed=16 << 20, transcendentals=0),
    )(info, sources, points, matrix)
    next_matrix = cross(next_points, next_sources, 1)
    updated = pl.pallas_call(
        update_kernel,
        out_shape=rows_out,
        in_specs=[SMEM, SMEM, VMEM, VMEM, VMEM],
        out_specs=VMEM,
        scratch_shapes=[pltpu.VMEM((PANEL, PANEL), f32)],
        compiler_params=PARAMS,
        name="update_kernel",
        cost_estimate=pl.CostEstimate(flops=10**10, bytes_accessed=16 << 20, transcendentals=0),
    )(info, next_sources, weights, next_rows, next_matrix)
    return (factor, updated)


def solution(mesh):
    in_specs = (P(("row", "sub"), None), P(), P())
    out_specs = (P(("row", "sub"), None), P(("row", "sub"), None))
    return jax.shard_map(body, mesh=mesh, in_specs=in_specs, out_specs=out_specs, check_vma=False)
```

```python
import math

import jax
import jax.numpy as jnp
from jax import lax
from jax.experimental import pallas as pl
from jax.experimental.pallas import tpu as pltpu
from jax.sharding import PartitionSpec as P

PANEL = 1024
DEPTH = 10
GROUP = 8
TILE = 128
STEPS = PANEL // TILE

weight_var = 2.0
bias_var = 0.1
noise_var = 0.1
f32 = jnp.float32
bf16 = jnp.bfloat16

ARC_A = 0.2353731889436501
ARC_B = 0.116208962721599
ARC_C = 3.2233309496295237
ARC_D = 0.005000674198862276


def nn(a, b):
    return lax.dot_general(a, b, (((1,), (0,)), ((), ())), preferred_element_type=f32)


def nt(a, b):
    return lax.dot_general(a, b, (((1,), (1,)), ((), ())), preferred_element_type=f32)


def split3(x):
    h = x.astype(bf16)
    r = x - h.astype(f32)
    m = r.astype(bf16)
    l = (r - m.astype(f32)).astype(bf16)
    return h, m, l


def lhs6(x):
    h, m, l = split3(x)
    return jnp.concatenate([h, m, h, m, h, l], 1)


def rhs6_nn(x):
    h, m, l = split3(x)
    return jnp.concatenate([h, h, m, m, l, h], 0)


def rhs6_nt(x):
    h, m, l = split3(x)
    return jnp.concatenate([h, h, m, m, l, h], 1)


def own_square(rows_ref, start):
    rows = rows_ref[start : start + TILE, :]
    gram = nt(rows, rows)
    eye = lax.broadcasted_iota(jnp.int32, (TILE, TILE), 0) == lax.broadcasted_iota(
        jnp.int32, (TILE, TILE), 1
    )
    only = jnp.where(eye, gram, 0.0)
    scale = weight_var / rows_ref.shape[1]
    return (
        jnp.sum(only, axis=0, keepdims=True) * scale + bias_var,
        jnp.sum(only, axis=1, keepdims=True) * scale + bias_var,
    )


def layer_scales(q):
    inv = [lax.rsqrt(q + bias_var * n) for n in range(DEPTH)]
    ratio = [(q + bias_var * n) * inv[n] * inv[n + 1] for n in range(DEPTH - 1)]
    offset = [inv[n + 1] * math.sqrt(bias_var) for n in range(DEPTH - 1)]
    last = (q + bias_var * (DEPTH - 1)) * inv[DEPTH - 1]
    return inv[0], ratio, offset, last


def store_columns(tab_ref, start, q):
    first, ratio, offset, last = layer_scales(q)
    for at, row in enumerate([first] + ratio + offset + [last]):
        tab_ref[at : at + 1, start : start + TILE] = row


def relu_layers(gram, q_rows, tab_ref, lo, width):
    scales = [layer_scales(q) for q in q_rows]
    pieces = range(width // TILE)
    col = lambda at, w: jnp.broadcast_to(
        tab_ref[at : at + 1, lo + w * TILE : lo + (w + 1) * TILE], (GROUP, TILE)
    )
    scale = weight_var / 3072
    c = [
        [
            (g[:, w * TILE : (w + 1) * TILE] * scale + bias_var) * (first * col(0, w))
            for w in pieces
        ]
        for g, (first, _, _, _) in zip(gram, scales)
    ]
    for n in range(DEPTH):
        for r, (_, ratio, offset, last) in enumerate(scales):
            for w in pieces:
                x = c[r][w]
                u = jnp.maximum(1.0 - (jnp.abs(x) if n == 0 else x), 1e-30)
                p = (ARC_D * u + ARC_A) + ARC_B * lax.rsqrt(ARC_C - u)
                g = (jnp.maximum(x, 0.0) if n == 0 else x) + (u * u) * lax.rsqrt(u) * p
                if n < DEPTH - 1:
                    c[r][w] = g * (ratio[n] * col(1 + n, w)) + offset[n] * col(DEPTH + n, w)
                else:
                    c[r][w] = g * (last * col(2 * DEPTH - 1, w)) + bias_var
    return [jnp.concatenate(row, axis=1) for row in c]


def total(xs):
    xs = list(xs)
    while len(xs) > 1:
        xs = [xs[i] + xs[i + 1] if i + 1 < len(xs) else xs[i] for i in range(0, len(xs), 2)]
    return xs[0]


def block_inverse(d_ref, cs_ref):
    lane = lax.broadcasted_iota(jnp.int32, (8, TILE), 1)
    sub = lax.broadcasted_iota(jnp.int32, (8, TILE), 0)
    spread = lambda x: jnp.broadcast_to(x, (8, TILE))
    now = d_ref[0:8, :]
    for s in range(TILE // 8):
        r0 = 8 * s
        slot = 64 * (s % 2)
        inside = (lane >= r0) & (lane < r0 + 8)
        for j in range(8):
            cs_ref[slot + 8 * j : slot + 8 * j + 8, :] = spread(now[:, r0 + j : r0 + j + 1])
        e = [
            [
                spread(cs_ref[slot + 8 * j + i : slot + 8 * j + i + 1, :]) if j >= i else None
                for j in range(8)
            ]
            for i in range(8)
        ]
        below = {}
        for i in range(s + 1, TILE // 8):
            b = d_ref[8 * i : 8 * i + 8, :]
            below[i] = (b, [spread(b[:, r0 + j : r0 + j + 1]) for j in range(8)])
        t = [
            jnp.where(inside, (lane == r0 + j).astype(f32), spread(d_ref[r0 + j : r0 + j + 1, :]))
            for j in range(8)
        ]
        w = [[None] * 8 for _ in range(8)]
        z = [None] * 8
        rows = [None] * 8
        for j in range(0, 8, 2):
            a, b, c = e[j][j], e[j][j + 1], e[j + 1][j + 1]
            root_det = lax.rsqrt(a * c - b * b)
            root_a = lax.rsqrt(a)
            rd = root_det * root_det
            for i in range(j + 2, 8):
                f0 = (c * e[j][i] - b * e[j + 1][i]) * rd
                f1 = (a * e[j + 1][i] - b * e[j][i]) * rd
                for q in range(i, 8):
                    e[i][q] = e[i][q] - (f0 * e[j][q] + f1 * e[j + 1][q])
                t[i] = t[i] - (f0 * t[j] + f1 * t[j + 1])
                for k in range(j):
                    w[i][k] = w[i][k] - (f0 * w[j][k] + f1 * w[j + 1][k])
                w[i][j], w[i][j + 1] = -f0, -f1
            z[j] = (c * t[j] - b * t[j + 1]) * rd
            z[j + 1] = (a * t[j + 1] - b * t[j]) * rd
            rows[j] = t[j] * root_a
            rows[j + 1] = (t[j + 1] - (b * (root_a * root_a)) * t[j]) * (root_det * (a * root_a))
        g = [total([z[k]] + [w[i][k] * z[i] for i in range(k // 2 * 2 + 2, 8)]) for k in range(8)]
        out = rows[7]
        for j in range(6, -1, -1):
            out = jnp.where(sub == j, rows[j], out)
        d_ref[r0 : r0 + 8, :] = out
        for i in range(s + 1, TILE // 8):
            b, c = below[i]
            acc = jnp.where(inside, 0.0, b) - total([c[j] * g[j] for j in range(8)])
            d_ref[8 * i : 8 * i + 8, :] = acc
            if i == s + 1:
                now = acc


def place_points(src_ref, raw_ref, p_ref):
    def place(b, carry):
        pair = [raw_ref[src_ref[2 * b + n]].astype(f32) for n in range(2)]
        at = pl.ds(pl.multiple_of(b * 2 * GROUP, 2 * GROUP), 2 * GROUP)
        p_ref[at, :] = jnp.concatenate(pair, axis=0).astype(bf16)
        return carry

    lax.fori_loop(0, PANEL // (2 * GROUP), place, 0)


def local_kernel(info_ref, x_ref, q_ref, p_ref, out_ref, tab_ref, after):
    for b in range(PANEL // 256):
        out_ref[:, b * 256 : (b + 1) * 256] = nt(x_ref[...], p_ref[b * 256 : (b + 1) * 256, :])
    start = info_ref[0] + after
    place = info_ref[1 + after] * GROUP
    column = lax.broadcasted_iota(jnp.int32, (GROUP, PANEL), 1)
    within = lax.broadcasted_iota(jnp.int32, (GROUP, PANEL), 0)

    def row_blocks(f, carry):
        rounds = [f * 4 + n for n in range(4)]
        at = [pl.ds(pl.multiple_of(r * GROUP, GROUP), GROUP) for r in rounds]
        k = relu_layers([out_ref[a, :] for a in at], [q_ref[a, :] for a in at], tab_ref, 0, PANEL)
        for r, a, rows in zip(rounds, at, k):
            own = (r == start) & (column == place + within)
            out_ref[a, :] = jnp.where(r >= start, rows + jnp.where(own, noise_var, 0.0), 0.0)
        return carry

    def clear(f, carry):
        out_ref[pl.ds(pl.multiple_of(f * 32, 32), 32), :] = jnp.zeros((32, PANEL), f32)
        return carry

    lax.fori_loop(0, start // 4, clear, 0)
    lax.fori_loop(start // 4, out_ref.shape[0] // 32, row_blocks, 0)


def cross_kernel(info_ref, src_ref, x_ref, q_ref, raw_ref, out_ref, p_ref, tab_ref, *, after):
    place_points(src_ref, raw_ref, p_ref)
    for b in range(STEPS):
        store_columns(tab_ref, b * TILE, own_square(p_ref, b * TILE)[0])
    local_kernel(info_ref, x_ref, q_ref, p_ref, out_ref, tab_ref, after)


def factor_kernel(
    info_ref, src_ref, raw_ref, k_ref, f_ref, g_ref, p_ref, a_ref, inv_ref, tab_ref, qrow_ref, d_ref, cs_ref
):
    place_points(src_ref, raw_ref, p_ref)
    for b in range(STEPS):
        along, down = own_square(p_ref, b * TILE)
        store_columns(tab_ref, b * TILE, along)
        qrow_ref[b * TILE : (b + 1) * TILE, :] = jnp.broadcast_to(down, (TILE, TILE))
    for b in range(PANEL // 256):
        lo = b * 256
        for c in range(b, PANEL // 256):
            a_ref[lo : lo + 256, c * 256 : (c + 1) * 256] = nt(
                p_ref[lo : lo + 256, :], p_ref[c * 256 : (c + 1) * 256, :]
            )
    for b in range(STEPS):
        lo = b * TILE
        width = PANEL - lo
        many = 4 if b < 4 else 8 if b < 7 else 16
        column = lax.broadcasted_iota(jnp.int32, (GROUP, width), 1) + lo
        within = lax.broadcasted_iota(jnp.int32, (GROUP, width), 0)

        def row_blocks(f, carry, lo=lo, width=width, many=many, column=column, within=within):
            starts = [pl.multiple_of(lo + (f * many + n) * GROUP, GROUP) for n in range(many)]
            at = [pl.ds(r, GROUP) for r in starts]
            k = relu_layers([a_ref[a, lo:] for a in at], [qrow_ref[a, :] for a in at], tab_ref, lo, width)
            for r, a, rows in zip(starts, at, k):
                a_ref[a, lo:] = rows + jnp.where(column == r + within, noise_var, 0.0)
            return carry

        lax.fori_loop(0, TILE // GROUP // many, row_blocks, 0)

    row = lax.broadcasted_iota(jnp.int32, (TILE, TILE), 0)
    col = lax.broadcasted_iota(jnp.int32, (TILE, TILE), 1)
    f_ref[...] = k_ref[...]

    def step(k, carry):
        k0 = pl.multiple_of(k * TILE, TILE)
        d_ref[...] = a_ref[pl.ds(k0, TILE), pl.ds(k0, TILE)]
        block_inverse(d_ref, cs_ref)
        linv = jnp.where(row >= col, d_ref[...], 0.0)
        inv_ref[k] = linv
        for kk in range(STEPS - 1):

            @pl.when(k == kk)
            def _():
                b0, c0 = kk * TILE, (kk + 1) * TILE
                u = nn(lhs6(linv), rhs6_nn(a_ref[b0:c0, c0:]))
                a_ref[b0:c0, c0:] = u
                u6 = rhs6_nn(u)
                for i in range(kk + 1, STEPS):
                    i0 = i * TILE
                    x = u[:, i0 - c0 : i0 - c0 + TILE].T
                    a_ref[i0 : i0 + TILE, i0:] = a_ref[i0 : i0 + TILE, i0:] - nn(
                        lhs6(x), u6[:, i0 - c0 :]
                    )

        return carry

    lax.fori_loop(0, STEPS, step, 0)

    for k in range(STEPS):
        b0, c0 = k * TILE, (k + 1) * TILE
        x = nt(lhs6(f_ref[:, b0:c0]), rhs6_nt(inv_ref[k]))
        f_ref[:, b0:c0] = x
        if k < STEPS - 1:
            f_ref[:, c0:] = f_ref[:, c0:] - nn(lhs6(x), rhs6_nn(a_ref[b0:c0, c0:]))

    at = pl.ds(pl.multiple_of(info_ref[0] * GROUP, GROUP), GROUP)
    column = lax.broadcasted_iota(jnp.int32, (GROUP, PANEL), 1)
    within = lax.broadcasted_iota(jnp.int32, (GROUP, PANEL), 0)
    f_ref[at, :] = jnp.where(column <= info_ref[1] * GROUP + within, f_ref[at, :], 0.0)

    g_ref[...] = f_ref[...]
    for k in range(STEPS - 1, -1, -1):
        b0, c0 = k * TILE, (k + 1) * TILE
        x = nn(lhs6(g_ref[:, b0:c0]), rhs6_nn(inv_ref[k]))
        g_ref[:, b0:c0] = x
        if k:
            g_ref[:, :b0] = g_ref[:, :b0] - nt(lhs6(x), rhs6_nt(a_ref[:b0, b0:c0]))


def update_kernel(info_ref, src_ref, g_ref, nk_ref, nl_ref, out_ref, kn_ref):
    def place(b, carry):
        at = pl.ds(pl.multiple_of(b * GROUP, GROUP), GROUP)
        kn_ref[at, :] = nk_ref[src_ref[b]]
        return carry

    lax.fori_loop(0, PANEL // GROUP, place, 0, unroll=8)
    rows = lax.broadcasted_iota(jnp.int32, (g_ref.shape[0], 256), 0) // GROUP
    live = rows > info_ref[0]
    for b in range(PANEL // 256):
        total = nl_ref[:, b * 256 : (b + 1) * 256]
        for k in range(STEPS):
            k0 = k * TILE
            total = total - nt(
                lhs6(g_ref[:, k0 : k0 + TILE]),
                rhs6_nt(kn_ref[b * 256 : (b + 1) * 256, k0 : k0 + TILE]),
            )
        out_ref[:, b * 256 : (b + 1) * 256] = jnp.where(live, total, 0.0)


ORDERS = (("x", "y", "z"), ("y", "z", "x"), ("z", "x", "y"))


def gather_kernel(block_ref, out_ref, near_send, near_recv, pair_send, pair_recv, own_sem, *, cuts):
    row, sub = lax.axis_index("row"), lax.axis_index("sub")
    me = {"z": row // 8, "y": row // 2 % 4, "x": sub}
    core = row % 2

    def device(at, core_at):
        return (at["z"] * 8 + at["y"] * 2 + core_at, at["x"])

    def shifted(axis, by):
        return {**me, axis: (me[axis] + by + 4) % 4}

    partner = device(me, 1 - core)
    peers = [device(shifted(a, by), core) for a in "zyx" for by in (1, -1)] + [partner]
    barrier = pltpu.get_barrier_semaphore()
    for peer in peers:
        pl.semaphore_signal(barrier, inc=1, device_id=peer, device_id_type=pl.DeviceIdType.MESH)
    pl.semaphore_wait(barrier, len(peers))

    def part(at, core_at, lo, hi):
        return out_ref.at[at["z"], at["y"], core_at, at["x"], :, lo:hi]

    def copy(src, dst, send, recv, to):
        return pltpu.make_async_remote_copy(
            src_ref=src,
            dst_ref=dst,
            send_sem=send,
            recv_sem=recv,
            device_id=to,
            device_id_type=pl.DeviceIdType.MESH,
        )

    every = pl.ds(0, 4)
    width = block_ref.shape[1]
    mine = pltpu.make_async_copy(block_ref, part(me, core, 0, width), own_sem)
    mine.start()
    sent = []

    def to_partner(at, lo, hi, slot):
        c = copy(part(at, core, lo, hi), part(at, core, lo, hi), pair_send.at[slot], pair_recv.at[slot], partner)
        c.start()
        arriving.append(
            copy(part(at, 1 - core, lo, hi), part(at, 1 - core, lo, hi), pair_send.at[slot], pair_recv.at[slot], partner)
        )
        sent.append(c)

    arriving = []
    for t in range(3):
        held = []
        for s, order in enumerate(ORDERS):
            lo, mid, hi = cuts[s]
            axis = order[t]
            sets = {
                by: {**{a: every if order.index(a) < t else me[a] for a in "zyx"}, axis: (me[axis] + by + 4) % 4}
                for by in (0, 1, -1, 2)
            }
            up, down = device(shifted(axis, 1), core), device(shifted(axis, -1), core)

            def near(kind, by, a, b, to, s=s, t=t, sets=sets):
                piece = part(sets[by], core, a, b)
                source = block_ref.at[:, a:b] if t == 0 and by == 0 else piece
                return copy(source, piece, near_send.at[s, t, kind], near_recv.at[s, t, kind], to)

            for kind, to in ((0, up), (1, down)):
                c = near(kind, 0, lo, hi, to)
                c.start()
                sent.append(c)
            held.append((near, sets, up, down, lo, mid, hi))
        if t == 0:
            mine.wait()
            to_partner(me, 0, width, 27)
        for s, (near, sets, up, down, lo, mid, hi) in enumerate(held):
            near(0, -1, lo, hi, up).wait_recv()
            c = near(2, -1, lo, mid, up)
            c.start()
            sent.append(c)
            near(1, 1, lo, hi, down).wait_recv()
            c = near(3, 1, mid, hi, down)
            c.start()
            sent.append(c)
            to_partner(sets[-1], lo, hi, 9 * s + 3 * t)
            to_partner(sets[1], lo, hi, 9 * s + 3 * t + 1)
        for s, (near, sets, up, down, lo, mid, hi) in enumerate(held):
            near(2, 2, lo, mid, up).wait_recv()
            near(3, 2, mid, hi, down).wait_recv()
            to_partner(sets[2], lo, hi, 9 * s + 3 * t + 2)
    for c in arriving:
        c.wait_recv()
    for c in sent:
        c.wait_send()


def gather_blocks(block, collective_id):
    rows, width = block.shape
    tiles = width // 128
    first = [0, tiles * 3 // 8 if tiles % 3 else tiles // 3, tiles * 3 // 4 if tiles % 3 else 2 * tiles // 3, tiles]
    cuts = [(128 * a, 128 * ((a + b + 1) // 2), 128 * b) for a, b in zip(first, first[1:])]
    out = pl.pallas_call(
        lambda *refs: gather_kernel(*refs, cuts=cuts),
        out_shape=jax.ShapeDtypeStruct((4, 4, 2, 4, rows, width), block.dtype),
        in_specs=[pl.BlockSpec(memory_space=pl.ANY)],
        out_specs=pl.BlockSpec(memory_space=pl.ANY),
        scratch_shapes=[
            pltpu.SemaphoreType.DMA((3, 3, 4)),
            pltpu.SemaphoreType.DMA((3, 3, 4)),
            pltpu.SemaphoreType.DMA((28,)),
            pltpu.SemaphoreType.DMA((28,)),
            pltpu.SemaphoreType.DMA,
        ],
        compiler_params=pltpu.CompilerParams(collective_id=collective_id, has_side_effects=True),
        name="gather_kernel",
    )(block)
    return out.reshape(128, rows, width)


SMEM = pl.BlockSpec(memory_space=pltpu.SMEM)
VMEM = pl.BlockSpec(memory_space=pltpu.VMEM)
PARAMS = pltpu.CompilerParams(vmem_limit_bytes=28 * 1024 * 1024)


def row_variance(rows):
    values = rows.astype(f32)
    return jnp.sum(values * values, axis=1) * (weight_var / rows.shape[1]) + bias_var


def body(images, block_id, panel_index):
    rows_dev, features = images.shape
    shards = lax.axis_size("row") * lax.axis_size("sub")
    myself = lax.axis_index("row") * lax.axis_size("sub") + lax.axis_index("sub")
    panel = panel_index[0]
    everyone = jnp.arange(shards, dtype=jnp.int32)
    local_var = jnp.broadcast_to(row_variance(images)[:, None], (rows_dev, TILE))

    def arrangement(which):
        positions = lax.dynamic_index_in_dim(block_id, which, 1, keepdims=False) - which * shards
        sources = jnp.sum(
            jnp.where(positions[None, :] == everyone[:, None], everyone[None, :], 0), axis=1
        )
        return sources, positions[myself]

    def gather(block):
        return lax.all_gather(block, ("row", "sub"), axis=0, tiled=True).reshape(
            shards, GROUP, -1
        )

    def own(which, array):
        return lax.dynamic_slice_in_dim(array, which * GROUP, GROUP, 0)

    sources, position = arrangement(panel)
    next_sources, next_position = arrangement(panel + 1)
    info = jnp.stack([panel, position, next_position])
    points = gather_blocks(own(panel, images), 0)
    next_points = gather(own(panel + 1, images))
    table = pltpu.VMEM((24, PANEL), f32)
    placed = pltpu.VMEM((PANEL, features), bf16)
    rows_out = jax.ShapeDtypeStruct((rows_dev, PANEL), f32)

    def cross(blocks, order, after):
        return pl.pallas_call(
            lambda *refs: cross_kernel(*refs, after=after),
            out_shape=rows_out,
            in_specs=[SMEM, SMEM, VMEM, VMEM, VMEM],
            out_specs=VMEM,
            scratch_shapes=[placed, table],
            compiler_params=PARAMS,
            name="cross_kernel",
            cost_estimate=pl.CostEstimate(flops=2 * 10**10, bytes_accessed=16 << 20, transcendentals=0),
        )(info, order, images, local_var, blocks)

    matrix = cross(points, sources, 0)
    next_rows = gather(own(panel + 1, matrix))
    factor, weights = pl.pallas_call(
        factor_kernel,
        out_shape=(rows_out, rows_out),
        in_specs=[SMEM, SMEM, VMEM, VMEM],
        out_specs=(VMEM, VMEM),
        scratch_shapes=[
            placed,
            pltpu.VMEM((PANEL, PANEL), f32),
            pltpu.VMEM((STEPS, TILE, TILE), f32),
            table,
            pltpu.VMEM((PANEL, TILE), f32),
            pltpu.VMEM((TILE, TILE), f32),
            pltpu.VMEM((TILE, TILE), f32),
        ],
        compiler_params=PARAMS,
        name="factor_kernel",
        cost_estimate=pl.CostEstimate(flops=10**11, bytes_accessed=16 << 20, transcendentals=0),
    )(info, sources, points, matrix)
    next_matrix = cross(next_points, next_sources, 1)
    updated = pl.pallas_call(
        update_kernel,
        out_shape=rows_out,
        in_specs=[SMEM, SMEM, VMEM, VMEM, VMEM],
        out_specs=VMEM,
        scratch_shapes=[pltpu.VMEM((PANEL, PANEL), f32)],
        compiler_params=PARAMS,
        name="update_kernel",
        cost_estimate=pl.CostEstimate(flops=10**10, bytes_accessed=16 << 20, transcendentals=0),
    )(info, next_sources, weights, next_rows, next_matrix)
    return (factor, updated)


def solution(mesh):
    in_specs = (P(("row", "sub"), None), P(), P())
    out_specs = (P(("row", "sub"), None), P(("row", "sub"), None))
    return jax.shard_map(body, mesh=mesh, in_specs=in_specs, out_specs=out_specs, check_vma=False)
```

```python
import math

import jax
import jax.numpy as jnp
from jax import lax
from jax.experimental import pallas as pl
from jax.experimental.pallas import tpu as pltpu
from jax.sharding import PartitionSpec as P

PANEL = 1024
DEPTH = 10
GROUP = 8
TILE = 128
STEPS = PANEL // TILE

weight_var = 2.0
bias_var = 0.1
noise_var = 0.1
f32 = jnp.float32
bf16 = jnp.bfloat16

ARC_A = 0.2353731889436501
ARC_B = 0.116208962721599
ARC_C = 3.2233309496295237
ARC_D = 0.005000674198862276


def nn(a, b):
    return lax.dot_general(a, b, (((1,), (0,)), ((), ())), preferred_element_type=f32)


def nt(a, b):
    return lax.dot_general(a, b, (((1,), (1,)), ((), ())), preferred_element_type=f32)


def split3(x):
    h = x.astype(bf16)
    r = x - h.astype(f32)
    m = r.astype(bf16)
    l = (r - m.astype(f32)).astype(bf16)
    return h, m, l


def lhs6(x):
    h, m, l = split3(x)
    return jnp.concatenate([h, m, h, m, h, l], 1)


def rhs6_nn(x):
    h, m, l = split3(x)
    return jnp.concatenate([h, h, m, m, l, h], 0)


def rhs6_nt(x):
    h, m, l = split3(x)
    return jnp.concatenate([h, h, m, m, l, h], 1)


def own_square(rows_ref, start):
    rows = rows_ref[start : start + TILE, :]
    gram = nt(rows, rows)
    eye = lax.broadcasted_iota(jnp.int32, (TILE, TILE), 0) == lax.broadcasted_iota(
        jnp.int32, (TILE, TILE), 1
    )
    only = jnp.where(eye, gram, 0.0)
    scale = weight_var / rows_ref.shape[1]
    return (
        jnp.sum(only, axis=0, keepdims=True) * scale + bias_var,
        jnp.sum(only, axis=1, keepdims=True) * scale + bias_var,
    )


def layer_scales(q):
    inv = [lax.rsqrt(q + bias_var * n) for n in range(DEPTH)]
    ratio = [(q + bias_var * n) * inv[n] * inv[n + 1] for n in range(DEPTH - 1)]
    offset = [inv[n + 1] * math.sqrt(bias_var) for n in range(DEPTH - 1)]
    last = (q + bias_var * (DEPTH - 1)) * inv[DEPTH - 1]
    return inv[0], ratio, offset, last


def store_columns(tab_ref, start, q):
    first, ratio, offset, last = layer_scales(q)
    for at, row in enumerate([first] + ratio + offset + [last]):
        tab_ref[at : at + 1, start : start + TILE] = row


def relu_layers(gram, q_rows, tab_ref, lo, width):
    scales = [layer_scales(q) for q in q_rows]
    pieces = range(width // TILE)
    col = lambda at, w: jnp.broadcast_to(
        tab_ref[at : at + 1, lo + w * TILE : lo + (w + 1) * TILE], (GROUP, TILE)
    )
    scale = weight_var / 3072
    c = [
        [
            (g[:, w * TILE : (w + 1) * TILE] * scale + bias_var) * (first * col(0, w))
            for w in pieces
        ]
        for g, (first, _, _, _) in zip(gram, scales)
    ]
    for n in range(DEPTH):
        for r, (_, ratio, offset, last) in enumerate(scales):
            for w in pieces:
                x = c[r][w]
                u = jnp.maximum(1.0 - (jnp.abs(x) if n == 0 else x), 1e-30)
                p = (ARC_D * u + ARC_A) + ARC_B * lax.rsqrt(ARC_C - u)
                g = (jnp.maximum(x, 0.0) if n == 0 else x) + (u * u) * lax.rsqrt(u) * p
                if n < DEPTH - 1:
                    c[r][w] = g * (ratio[n] * col(1 + n, w)) + offset[n] * col(DEPTH + n, w)
                else:
                    c[r][w] = g * (last * col(2 * DEPTH - 1, w)) + bias_var
    return [jnp.concatenate(row, axis=1) for row in c]


def total(xs):
    xs = list(xs)
    while len(xs) > 1:
        xs = [xs[i] + xs[i + 1] if i + 1 < len(xs) else xs[i] for i in range(0, len(xs), 2)]
    return xs[0]


def block_inverse(d_ref, cs_ref):
    lane = lax.broadcasted_iota(jnp.int32, (8, TILE), 1)
    sub = lax.broadcasted_iota(jnp.int32, (8, TILE), 0)
    spread = lambda x: jnp.broadcast_to(x, (8, TILE))
    now = d_ref[0:8, :]
    for s in range(TILE // 8):
        r0 = 8 * s
        slot = 64 * (s % 2)
        inside = (lane >= r0) & (lane < r0 + 8)
        for j in range(8):
            cs_ref[slot + 8 * j : slot + 8 * j + 8, :] = spread(now[:, r0 + j : r0 + j + 1])
        e = [
            [
                spread(cs_ref[slot + 8 * j + i : slot + 8 * j + i + 1, :]) if j >= i else None
                for j in range(8)
            ]
            for i in range(8)
        ]
        below = {}
        for i in range(s + 1, TILE // 8):
            b = d_ref[8 * i : 8 * i + 8, :]
            below[i] = (b, [spread(b[:, r0 + j : r0 + j + 1]) for j in range(8)])
        t = [
            jnp.where(inside, (lane == r0 + j).astype(f32), spread(d_ref[r0 + j : r0 + j + 1, :]))
            for j in range(8)
        ]
        w = [[None] * 8 for _ in range(8)]
        z = [None] * 8
        rows = [None] * 8
        for j in range(0, 8, 2):
            a, b, c = e[j][j], e[j][j + 1], e[j + 1][j + 1]
            root_det = lax.rsqrt(a * c - b * b)
            root_a = lax.rsqrt(a)
            rd = root_det * root_det
            for i in range(j + 2, 8):
                f0 = (c * e[j][i] - b * e[j + 1][i]) * rd
                f1 = (a * e[j + 1][i] - b * e[j][i]) * rd
                for q in range(i, 8):
                    e[i][q] = e[i][q] - (f0 * e[j][q] + f1 * e[j + 1][q])
                t[i] = t[i] - (f0 * t[j] + f1 * t[j + 1])
                for k in range(j):
                    w[i][k] = w[i][k] - (f0 * w[j][k] + f1 * w[j + 1][k])
                w[i][j], w[i][j + 1] = -f0, -f1
            z[j] = (c * t[j] - b * t[j + 1]) * rd
            z[j + 1] = (a * t[j + 1] - b * t[j]) * rd
            rows[j] = t[j] * root_a
            rows[j + 1] = (t[j + 1] - (b * (root_a * root_a)) * t[j]) * (root_det * (a * root_a))
        g = [total([z[k]] + [w[i][k] * z[i] for i in range(k // 2 * 2 + 2, 8)]) for k in range(8)]
        out = rows[7]
        for j in range(6, -1, -1):
            out = jnp.where(sub == j, rows[j], out)
        d_ref[r0 : r0 + 8, :] = out
        for i in range(s + 1, TILE // 8):
            b, c = below[i]
            acc = jnp.where(inside, 0.0, b) - total([c[j] * g[j] for j in range(8)])
            d_ref[8 * i : 8 * i + 8, :] = acc
            if i == s + 1:
                now = acc


def place_points(src_ref, raw_ref, p_ref):
    def place(b, carry):
        pair = [raw_ref[src_ref[2 * b + n]].astype(f32) for n in range(2)]
        at = pl.ds(pl.multiple_of(b * 2 * GROUP, 2 * GROUP), 2 * GROUP)
        p_ref[at, :] = jnp.concatenate(pair, axis=0).astype(bf16)
        return carry

    lax.fori_loop(0, PANEL // (2 * GROUP), place, 0)


def local_kernel(info_ref, x_ref, q_ref, p_ref, out_ref, tab_ref, after):
    for b in range(x_ref.shape[0] // TILE):
        down = own_square(x_ref, b * TILE)[1]
        q_ref[b * TILE : (b + 1) * TILE, :] = jnp.broadcast_to(down, (TILE, TILE))
    for b in range(PANEL // 256):
        out_ref[:, b * 256 : (b + 1) * 256] = nt(x_ref[...], p_ref[b * 256 : (b + 1) * 256, :])
    start = info_ref[0] + after
    place = info_ref[1 + after] * GROUP
    column = lax.broadcasted_iota(jnp.int32, (GROUP, PANEL), 1)
    within = lax.broadcasted_iota(jnp.int32, (GROUP, PANEL), 0)

    def row_blocks(f, carry):
        rounds = [f * 4 + n for n in range(4)]
        at = [pl.ds(pl.multiple_of(r * GROUP, GROUP), GROUP) for r in rounds]
        k = relu_layers([out_ref[a, :] for a in at], [q_ref[a, :] for a in at], tab_ref, 0, PANEL)
        for r, a, rows in zip(rounds, at, k):
            own = (r == start) & (column == place + within)
            out_ref[a, :] = jnp.where(r >= start, rows + jnp.where(own, noise_var, 0.0), 0.0)
        return carry

    def clear(f, carry):
        out_ref[pl.ds(pl.multiple_of(f * 32, 32), 32), :] = jnp.zeros((32, PANEL), f32)
        return carry

    lax.fori_loop(0, start // 4, clear, 0)
    lax.fori_loop(start // 4, out_ref.shape[0] // 32, row_blocks, 0)


def cross_kernel(info_ref, src_ref, x_ref, raw_ref, out_ref, *refs, after):
    block_ref, p_ref, tab_ref, q_ref = refs if after == 0 else (None, *refs)
    place_points(src_ref, raw_ref, p_ref)
    for b in range(STEPS):
        store_columns(tab_ref, b * TILE, own_square(p_ref, b * TILE)[0])
    local_kernel(info_ref, x_ref, q_ref, p_ref, out_ref, tab_ref, after)
    if after == 0:
        at = pl.multiple_of((info_ref[0] + 1) * GROUP, GROUP)
        block_ref[...] = out_ref[pl.ds(at, GROUP), :]


def diagonal_kernel(src_ref, raw_ref, block_ref, a_ref, all_ref, p_ref, tab_ref, qrow_ref, *sems):
    steps = iter(gather_steps(block_ref, all_ref, *sems))
    step = lambda: next(steps)()
    step()
    place_points(src_ref, raw_ref, p_ref)
    for b in range(STEPS):
        along, down = own_square(p_ref, b * TILE)
        store_columns(tab_ref, b * TILE, along)
        qrow_ref[b * TILE : (b + 1) * TILE, :] = jnp.broadcast_to(down, (TILE, TILE))
    step()
    for b in range(PANEL // 256):
        lo = b * 256
        for c in range(b, PANEL // 256):
            a_ref[lo : lo + 256, c * 256 : (c + 1) * 256] = nt(
                p_ref[lo : lo + 256, :], p_ref[c * 256 : (c + 1) * 256, :]
            )
        if b == 0:
            step()
    step()
    for b in range(STEPS):
        lo = b * TILE
        width = PANEL - lo
        many = 4 if b < 4 else 8 if b < 7 else 16
        column = lax.broadcasted_iota(jnp.int32, (GROUP, width), 1) + lo
        within = lax.broadcasted_iota(jnp.int32, (GROUP, width), 0)

        def row_blocks(f, carry, lo=lo, width=width, many=many, column=column, within=within):
            starts = [pl.multiple_of(lo + (f * many + n) * GROUP, GROUP) for n in range(many)]
            at = [pl.ds(r, GROUP) for r in starts]
            k = relu_layers([a_ref[a, lo:] for a in at], [qrow_ref[a, :] for a in at], tab_ref, lo, width)
            for r, a, rows in zip(starts, at, k):
                a_ref[a, lo:] = rows + jnp.where(column == r + within, noise_var, 0.0)
            return carry

        lax.fori_loop(0, TILE // GROUP // many, row_blocks, 0)
        if b in (0, 2, 5):
            step()
    step()


def factor_kernel(info_ref, m_ref, k_ref, f_ref, g_ref, a_ref, inv_ref, d_ref, cs_ref):
    a_ref[...] = m_ref[...]
    row = lax.broadcasted_iota(jnp.int32, (TILE, TILE), 0)
    col = lax.broadcasted_iota(jnp.int32, (TILE, TILE), 1)
    f_ref[...] = k_ref[...]

    def step(k, carry):
        k0 = pl.multiple_of(k * TILE, TILE)
        d_ref[...] = a_ref[pl.ds(k0, TILE), pl.ds(k0, TILE)]
        block_inverse(d_ref, cs_ref)
        linv = jnp.where(row >= col, d_ref[...], 0.0)
        inv_ref[k] = linv
        for kk in range(STEPS - 1):

            @pl.when(k == kk)
            def _():
                b0, c0 = kk * TILE, (kk + 1) * TILE
                u = nn(lhs6(linv), rhs6_nn(a_ref[b0:c0, c0:]))
                a_ref[b0:c0, c0:] = u
                u6 = rhs6_nn(u)
                for i in range(kk + 1, STEPS):
                    i0 = i * TILE
                    x = u[:, i0 - c0 : i0 - c0 + TILE].T
                    a_ref[i0 : i0 + TILE, i0:] = a_ref[i0 : i0 + TILE, i0:] - nn(
                        lhs6(x), u6[:, i0 - c0 :]
                    )

        return carry

    lax.fori_loop(0, STEPS, step, 0)

    for k in range(STEPS):
        b0, c0 = k * TILE, (k + 1) * TILE
        x = nt(lhs6(f_ref[:, b0:c0]), rhs6_nt(inv_ref[k]))
        f_ref[:, b0:c0] = x
        if k < STEPS - 1:
            f_ref[:, c0:] = f_ref[:, c0:] - nn(lhs6(x), rhs6_nn(a_ref[b0:c0, c0:]))

    at = pl.ds(pl.multiple_of(info_ref[0] * GROUP, GROUP), GROUP)
    column = lax.broadcasted_iota(jnp.int32, (GROUP, PANEL), 1)
    within = lax.broadcasted_iota(jnp.int32, (GROUP, PANEL), 0)
    f_ref[at, :] = jnp.where(column <= info_ref[1] * GROUP + within, f_ref[at, :], 0.0)

    g_ref[...] = f_ref[...]
    for k in range(STEPS - 1, -1, -1):
        b0, c0 = k * TILE, (k + 1) * TILE
        x = nn(lhs6(g_ref[:, b0:c0]), rhs6_nn(inv_ref[k]))
        g_ref[:, b0:c0] = x
        if k:
            g_ref[:, :b0] = g_ref[:, :b0] - nt(lhs6(x), rhs6_nt(a_ref[:b0, b0:c0]))


def update_kernel(info_ref, src_ref, g_ref, nk_ref, nl_ref, out_ref, kn_ref):
    def place(b, carry):
        at = pl.ds(pl.multiple_of(b * GROUP, GROUP), GROUP)
        kn_ref[at, :] = nk_ref[src_ref[b]]
        return carry

    lax.fori_loop(0, PANEL // GROUP, place, 0, unroll=8)
    rows = lax.broadcasted_iota(jnp.int32, (g_ref.shape[0], 256), 0) // GROUP
    live = rows > info_ref[0]
    for b in range(PANEL // 256):
        total = nl_ref[:, b * 256 : (b + 1) * 256]
        for k in range(STEPS):
            k0 = k * TILE
            total = total - nt(
                lhs6(g_ref[:, k0 : k0 + TILE]),
                rhs6_nt(kn_ref[b * 256 : (b + 1) * 256, k0 : k0 + TILE]),
            )
        out_ref[:, b * 256 : (b + 1) * 256] = jnp.where(live, total, 0.0)


ORDERS = (("x", "y", "z"), ("y", "z", "x"), ("z", "x", "y"))


def gather_steps(block_ref, out_ref, near_send, near_recv, pair_send, pair_recv, own_sem):
    row, sub = lax.axis_index("row"), lax.axis_index("sub")
    me = {"z": row // 8, "y": row // 2 % 4, "x": sub}
    core = row % 2
    width = block_ref.shape[1]
    tiles = width // TILE
    first = [0, (tiles * 3 + 7) // 8, (tiles * 3 + 3) // 4, tiles] if tiles % 3 else [n * tiles // 3 for n in range(4)]
    cuts = [(TILE * a, TILE * ((a + b + 1) // 2), TILE * b) for a, b in zip(first, first[1:])]
    every = pl.ds(0, 4)

    def device(at, core_at):
        return (at["z"] * 8 + at["y"] * 2 + core_at, at["x"])

    def shifted(axis, by):
        return {**me, axis: (me[axis] + by + 4) % 4}

    partner = device(me, 1 - core)
    sent, arriving = [], []

    def part(at, core_at, lo, hi):
        return out_ref.at[at["z"], at["y"], core_at, at["x"], :, lo:hi]

    def copy(src, dst, send, recv, to):
        return pltpu.make_async_remote_copy(
            src_ref=src,
            dst_ref=dst,
            send_sem=send,
            recv_sem=recv,
            device_id=to,
            device_id_type=pl.DeviceIdType.MESH,
        )

    def to_partner(at, lo, hi, slot):
        ours, theirs = part(at, core, lo, hi), part(at, 1 - core, lo, hi)
        c = copy(ours, ours, pair_send.at[slot], pair_recv.at[slot], partner)
        c.start()
        sent.append(c)
        arriving.append(copy(theirs, theirs, pair_send.at[slot], pair_recv.at[slot], partner))

    def sets(s, t, by):
        order = ORDERS[s]
        axis = order[t]
        return {
            **{a: every if order.index(a) < t else me[a] for a in "zyx"},
            axis: (me[axis] + by + 4) % 4,
        }

    def near(s, t, kind, end):
        lo, mid, hi = cuts[s]
        lo, hi = ((lo, hi), (lo, hi), (lo, mid), (mid, hi))[kind]
        to = device(shifted(ORDERS[s][t], 1 if kind in (0, 2) else -1), core)

        def along(by):
            piece = part(sets(s, t, by), core, lo, hi)
            source = block_ref.at[:, lo:hi] if t == 0 and by == 0 else piece
            return copy(source, piece, near_send.at[s, t, kind], near_recv.at[s, t, kind], to)

        return along(((0, 0, -1, 1), (-1, 1, 2, 2))[end][kind])

    def send(s, t, kind):
        c = near(s, t, kind, 0)
        c.start()
        sent.append(c)

    def begin(t):
        for s in range(3):
            send(s, t, 0)
            send(s, t, 1)

    mine = pltpu.make_async_copy(block_ref, part(me, core, 0, width), own_sem)

    def enter():
        peers = [device(shifted(a, by), core) for a in "zyx" for by in (1, -1)] + [partner]
        barrier = pltpu.get_barrier_semaphore()
        for peer in peers:
            pl.semaphore_signal(barrier, inc=1, device_id=peer, device_id_type=pl.DeviceIdType.MESH)
        pl.semaphore_wait(barrier, len(peers))
        mine.start()
        begin(0)

    def pass_on(t):
        if t == 0:
            mine.wait()
            to_partner(me, 0, width, 27)
        for s in range(3):
            for kind in (0, 1):
                near(s, t, kind, 1).wait_recv()
                send(s, t, 2 + kind)
        for s in range(3):
            lo, _, hi = cuts[s]
            to_partner(sets(s, t, -1), lo, hi, 9 * s + 3 * t)
            to_partner(sets(s, t, 1), lo, hi, 9 * s + 3 * t + 1)

    def complete(t):
        for s in range(3):
            for kind in (2, 3):
                near(s, t, kind, 1).wait_recv()
        if t < 2:
            begin(t + 1)
        for s in range(3):
            lo, _, hi = cuts[s]
            to_partner(sets(s, t, 2), lo, hi, 9 * s + 3 * t + 2)

    def leave():
        for c in arriving:
            c.wait_recv()
        for c in sent:
            c.wait_send()

    steps = [enter]
    for t in range(3):
        steps += [lambda t=t: pass_on(t), lambda t=t: complete(t)]
    return steps + [leave]


GATHER_SCRATCH = [
    pltpu.SemaphoreType.DMA((3, 3, 4)),
    pltpu.SemaphoreType.DMA((3, 3, 4)),
    pltpu.SemaphoreType.DMA((28,)),
    pltpu.SemaphoreType.DMA((28,)),
    pltpu.SemaphoreType.DMA,
]


def gather_kernel(*refs):
    for step in gather_steps(*refs):
        step()


def gather_blocks(block, collective_id):
    rows, width = block.shape
    out = pl.pallas_call(
        gather_kernel,
        out_shape=jax.ShapeDtypeStruct((4, 4, 2, 4, rows, width), block.dtype),
        in_specs=[VMEM],
        out_specs=ANY,
        scratch_shapes=GATHER_SCRATCH,
        compiler_params=pltpu.CompilerParams(collective_id=collective_id, has_side_effects=True),
        name="gather_kernel",
    )(block)
    return out.reshape(128, rows, width)


SMEM = pl.BlockSpec(memory_space=pltpu.SMEM)
VMEM = pl.BlockSpec(memory_space=pltpu.VMEM)
ANY = pl.BlockSpec(memory_space=pl.ANY)
PARAMS = pltpu.CompilerParams(vmem_limit_bytes=28 * 1024 * 1024)


def body(images, block_id, panel_index):
    rows_dev, features = images.shape
    shards = lax.axis_size("row") * lax.axis_size("sub")
    myself = lax.axis_index("row") * lax.axis_size("sub") + lax.axis_index("sub")
    panel = panel_index[0]
    everyone = jnp.arange(shards, dtype=jnp.int32)

    def arrangement(which):
        positions = lax.dynamic_index_in_dim(block_id, which, 1, keepdims=False) - which * shards
        sources = jnp.sum(
            jnp.where(positions[None, :] == everyone[:, None], everyone[None, :], 0), axis=1
        )
        return sources, positions[myself]

    def gather(block):
        return lax.all_gather(block, ("row", "sub"), axis=0, tiled=True).reshape(
            shards, GROUP, -1
        )

    def own(which, array):
        return lax.dynamic_slice_in_dim(array, which * GROUP, GROUP, 0)

    sources, position = arrangement(panel)
    next_sources, next_position = arrangement(panel + 1)
    info = jnp.stack([panel, position, next_position])
    points = gather_blocks(own(panel, images), 0)
    next_points = gather(own(panel + 1, images))
    table = pltpu.VMEM((24, PANEL), f32)
    placed = pltpu.VMEM((PANEL, features), bf16)
    rows_out = jax.ShapeDtypeStruct((rows_dev, PANEL), f32)

    def cross(blocks, order, after):
        return pl.pallas_call(
            lambda *refs: cross_kernel(*refs, after=after),
            out_shape=rows_out if after else (rows_out, jax.ShapeDtypeStruct((GROUP, PANEL), f32)),
            in_specs=[SMEM, SMEM, VMEM, VMEM],
            out_specs=VMEM if after else (VMEM, VMEM),
            scratch_shapes=[placed, table, pltpu.VMEM((rows_dev, TILE), f32)],
            compiler_params=PARAMS,
            name="cross_kernel",
            cost_estimate=pl.CostEstimate(flops=2 * 10**10, bytes_accessed=16 << 20, transcendentals=0),
        )(info, order, images, blocks)

    matrix, own_next = cross(points, sources, 0)
    diagonal, next_rows = pl.pallas_call(
        diagonal_kernel,
        out_shape=(
            jax.ShapeDtypeStruct((PANEL, PANEL), f32),
            jax.ShapeDtypeStruct((4, 4, 2, 4, GROUP, PANEL), f32),
        ),
        in_specs=[SMEM, VMEM, VMEM],
        out_specs=(VMEM, ANY),
        scratch_shapes=[placed, table, pltpu.VMEM((PANEL, TILE), f32)] + GATHER_SCRATCH,
        compiler_params=pltpu.CompilerParams(
            vmem_limit_bytes=48 * 1024 * 1024, collective_id=1, has_side_effects=True
        ),
        name="diagonal_kernel",
        cost_estimate=pl.CostEstimate(flops=3 * 10**10, bytes_accessed=16 << 20, transcendentals=0),
    )(sources, points, own_next)
    next_rows = next_rows.reshape(shards, GROUP, PANEL)
    factor, weights = pl.pallas_call(
        factor_kernel,
        out_shape=(rows_out, rows_out),
        in_specs=[SMEM, VMEM, VMEM],
        out_specs=(VMEM, VMEM),
        scratch_shapes=[
            pltpu.VMEM((PANEL, PANEL), f32),
            pltpu.VMEM((STEPS, TILE, TILE), f32),
            pltpu.VMEM((TILE, TILE), f32),
            pltpu.VMEM((TILE, TILE), f32),
        ],
        compiler_params=PARAMS,
        name="factor_kernel",
        cost_estimate=pl.CostEstimate(flops=10**11, bytes_accessed=16 << 20, transcendentals=0),
    )(info, diagonal, matrix)
    next_matrix = cross(next_points, next_sources, 1)
    updated = pl.pallas_call(
        update_kernel,
        out_shape=rows_out,
        in_specs=[SMEM, SMEM, VMEM, VMEM, VMEM],
        out_specs=VMEM,
        scratch_shapes=[pltpu.VMEM((PANEL, PANEL), f32)],
        compiler_params=PARAMS,
        name="update_kernel",
        cost_estimate=pl.CostEstimate(flops=10**10, bytes_accessed=16 << 20, transcendentals=0),
    )(info, next_sources, weights, next_rows, next_matrix)
    return (factor, updated)


def solution(mesh):
    in_specs = (P(("row", "sub"), None), P(), P())
    out_specs = (P(("row", "sub"), None), P(("row", "sub"), None))
    return jax.shard_map(body, mesh=mesh, in_specs=in_specs, out_specs=out_specs, check_vma=False)
```

```python
import math

import jax
import jax.numpy as jnp
from jax import lax
from jax.experimental import pallas as pl
from jax.experimental.pallas import tpu as pltpu
from jax.sharding import PartitionSpec as P

PANEL = 1024
DEPTH = 10
GROUP = 8
TILE = 128
STEPS = PANEL // TILE

weight_var = 2.0
bias_var = 0.1
noise_var = 0.1
f32 = jnp.float32
bf16 = jnp.bfloat16

ARC_A = 0.2353731889436501
ARC_B = 0.116208962721599
ARC_C = 3.2233309496295237
ARC_D = 0.005000674198862276


def nn(a, b):
    return lax.dot_general(a, b, (((1,), (0,)), ((), ())), preferred_element_type=f32)


def nt(a, b):
    return lax.dot_general(a, b, (((1,), (1,)), ((), ())), preferred_element_type=f32)


def split3(x):
    h = x.astype(bf16)
    r = x - h.astype(f32)
    m = r.astype(bf16)
    l = (r - m.astype(f32)).astype(bf16)
    return h, m, l


def lhs6(x):
    h, m, l = split3(x)
    return jnp.concatenate([h, m, h, m, h, l], 1)


def rhs6_nn(x):
    h, m, l = split3(x)
    return jnp.concatenate([h, h, m, m, l, h], 0)


def rhs6_nt(x):
    h, m, l = split3(x)
    return jnp.concatenate([h, h, m, m, l, h], 1)


def own_square(rows_ref, start):
    rows = rows_ref[start : start + TILE, :]
    gram = nt(rows, rows)
    eye = lax.broadcasted_iota(jnp.int32, (TILE, TILE), 0) == lax.broadcasted_iota(
        jnp.int32, (TILE, TILE), 1
    )
    only = jnp.where(eye, gram, 0.0)
    scale = weight_var / rows_ref.shape[1]
    return (
        jnp.sum(only, axis=0, keepdims=True) * scale + bias_var,
        jnp.sum(only, axis=1, keepdims=True) * scale + bias_var,
    )


def layer_scales(q):
    inv = [lax.rsqrt(q + bias_var * n) for n in range(DEPTH)]
    ratio = [(q + bias_var * n) * inv[n] * inv[n + 1] for n in range(DEPTH - 1)]
    offset = [inv[n + 1] * math.sqrt(bias_var) for n in range(DEPTH - 1)]
    last = (q + bias_var * (DEPTH - 1)) * inv[DEPTH - 1]
    return inv[0], ratio, offset, last


def store_columns(tab_ref, start, q):
    first, ratio, offset, last = layer_scales(q)
    for at, row in enumerate([first] + ratio + offset + [last]):
        tab_ref[at : at + 1, start : start + TILE] = row


def relu_layers(gram, q_rows, tab_ref, lo, width):
    scales = [layer_scales(q) for q in q_rows]
    pieces = range(width // TILE)
    col = lambda at, w: jnp.broadcast_to(
        tab_ref[at : at + 1, lo + w * TILE : lo + (w + 1) * TILE], (GROUP, TILE)
    )
    scale = weight_var / 3072
    c = [
        [
            (g[:, w * TILE : (w + 1) * TILE] * scale + bias_var) * (first * col(0, w))
            for w in pieces
        ]
        for g, (first, _, _, _) in zip(gram, scales)
    ]
    for n in range(DEPTH):
        for r, (_, ratio, offset, last) in enumerate(scales):
            for w in pieces:
                x = c[r][w]
                u = jnp.maximum(1.0 - (jnp.abs(x) if n == 0 else x), 1e-30)
                p = (ARC_D * u + ARC_A) + ARC_B * lax.rsqrt(ARC_C - u)
                g = (jnp.maximum(x, 0.0) if n == 0 else x) + (u * u) * lax.rsqrt(u) * p
                if n < DEPTH - 1:
                    c[r][w] = g * (ratio[n] * col(1 + n, w)) + offset[n] * col(DEPTH + n, w)
                else:
                    c[r][w] = g * (last * col(2 * DEPTH - 1, w)) + bias_var
    return [jnp.concatenate(row, axis=1) for row in c]


def total(xs):
    xs = list(xs)
    while len(xs) > 1:
        xs = [xs[i] + xs[i + 1] if i + 1 < len(xs) else xs[i] for i in range(0, len(xs), 2)]
    return xs[0]


def block_inverse(d_ref, cs_ref):
    lane = lax.broadcasted_iota(jnp.int32, (8, TILE), 1)
    sub = lax.broadcasted_iota(jnp.int32, (8, TILE), 0)
    spread = lambda x: jnp.broadcast_to(x, (8, TILE))
    now = d_ref[0:8, :]
    for s in range(TILE // 8):
        r0 = 8 * s
        slot = 64 * (s % 2)
        inside = (lane >= r0) & (lane < r0 + 8)
        for j in range(8):
            cs_ref[slot + 8 * j : slot + 8 * j + 8, :] = spread(now[:, r0 + j : r0 + j + 1])
        e = [
            [
                spread(cs_ref[slot + 8 * j + i : slot + 8 * j + i + 1, :]) if j >= i else None
                for j in range(8)
            ]
            for i in range(8)
        ]
        below = {}
        for i in range(s + 1, TILE // 8):
            b = d_ref[8 * i : 8 * i + 8, :]
            below[i] = (b, [spread(b[:, r0 + j : r0 + j + 1]) for j in range(8)])
        t = [
            jnp.where(inside, (lane == r0 + j).astype(f32), spread(d_ref[r0 + j : r0 + j + 1, :]))
            for j in range(8)
        ]
        w = [[None] * 8 for _ in range(8)]
        z = [None] * 8
        rows = [None] * 8
        for j in range(0, 8, 2):
            a, b, c = e[j][j], e[j][j + 1], e[j + 1][j + 1]
            root_det = lax.rsqrt(a * c - b * b)
            root_a = lax.rsqrt(a)
            rd = root_det * root_det
            for i in range(j + 2, 8):
                f0 = (c * e[j][i] - b * e[j + 1][i]) * rd
                f1 = (a * e[j + 1][i] - b * e[j][i]) * rd
                for q in range(i, 8):
                    e[i][q] = e[i][q] - (f0 * e[j][q] + f1 * e[j + 1][q])
                t[i] = t[i] - (f0 * t[j] + f1 * t[j + 1])
                for k in range(j):
                    w[i][k] = w[i][k] - (f0 * w[j][k] + f1 * w[j + 1][k])
                w[i][j], w[i][j + 1] = -f0, -f1
            z[j] = (c * t[j] - b * t[j + 1]) * rd
            z[j + 1] = (a * t[j + 1] - b * t[j]) * rd
            rows[j] = t[j] * root_a
            rows[j + 1] = (t[j + 1] - (b * (root_a * root_a)) * t[j]) * (root_det * (a * root_a))
        g = [total([z[k]] + [w[i][k] * z[i] for i in range(k // 2 * 2 + 2, 8)]) for k in range(8)]
        out = rows[7]
        for j in range(6, -1, -1):
            out = jnp.where(sub == j, rows[j], out)
        d_ref[r0 : r0 + 8, :] = out
        for i in range(s + 1, TILE // 8):
            b, c = below[i]
            acc = jnp.where(inside, 0.0, b) - total([c[j] * g[j] for j in range(8)])
            d_ref[8 * i : 8 * i + 8, :] = acc
            if i == s + 1:
                now = acc


def place_points(src_ref, raw_ref, p_ref):
    def place(b, carry):
        pair = [raw_ref[src_ref[2 * b + n]].astype(f32) for n in range(2)]
        at = pl.ds(pl.multiple_of(b * 2 * GROUP, 2 * GROUP), 2 * GROUP)
        p_ref[at, :] = jnp.concatenate(pair, axis=0).astype(bf16)
        return carry

    lax.fori_loop(0, PANEL // (2 * GROUP), place, 0)


def local_kernel(info_ref, x_ref, q_ref, p_ref, out_ref, tab_ref, after):
    for b in range(x_ref.shape[0] // TILE):
        down = own_square(x_ref, b * TILE)[1]
        q_ref[b * TILE : (b + 1) * TILE, :] = jnp.broadcast_to(down, (TILE, TILE))
    for b in range(PANEL // 256):
        out_ref[:, b * 256 : (b + 1) * 256] = nt(x_ref[...], p_ref[b * 256 : (b + 1) * 256, :])
    start = info_ref[0] + after
    place = info_ref[1 + after] * GROUP
    column = lax.broadcasted_iota(jnp.int32, (GROUP, PANEL), 1)
    within = lax.broadcasted_iota(jnp.int32, (GROUP, PANEL), 0)

    def row_blocks(f, carry):
        rounds = [f * 4 + n for n in range(4)]
        at = [pl.ds(pl.multiple_of(r * GROUP, GROUP), GROUP) for r in rounds]
        k = relu_layers([out_ref[a, :] for a in at], [q_ref[a, :] for a in at], tab_ref, 0, PANEL)
        for r, a, rows in zip(rounds, at, k):
            own = (r == start) & (column == place + within)
            out_ref[a, :] = jnp.where(r >= start, rows + jnp.where(own, noise_var, 0.0), 0.0)
        return carry

    def clear(f, carry):
        out_ref[pl.ds(pl.multiple_of(f * 32, 32), 32), :] = jnp.zeros((32, PANEL), f32)
        return carry

    lax.fori_loop(0, start // 4, clear, 0)
    lax.fori_loop(start // 4, out_ref.shape[0] // 32, row_blocks, 0)


def cross_kernel(info_ref, src_ref, x_ref, raw_ref, out_ref, p_ref, tab_ref, q_ref):
    place_points(src_ref, raw_ref, p_ref)
    for b in range(STEPS):
        store_columns(tab_ref, b * TILE, own_square(p_ref, b * TILE)[0])
    local_kernel(info_ref, x_ref, q_ref, p_ref, out_ref, tab_ref, 1)


def local_products(x_ref, p_ref, q_ref, out_ref):
    for b in range(x_ref.shape[0] // TILE):
        down = own_square(x_ref, b * TILE)[1]
        q_ref[b * TILE : (b + 1) * TILE, :] = jnp.broadcast_to(down, (TILE, TILE))
    for b in range(PANEL // 256):
        out_ref[:, b * 256 : (b + 1) * 256] = nt(x_ref[...], p_ref[b * 256 : (b + 1) * 256, :])


def own_rows_kernel(info_ref, src_ref, x_ref, raw_ref, block_ref, p_ref, tab_ref, q_ref, gram_ref):
    place_points(src_ref, raw_ref, p_ref)
    for b in range(STEPS):
        store_columns(tab_ref, b * TILE, own_square(p_ref, b * TILE)[0])
    local_products(x_ref, p_ref, q_ref, gram_ref)
    at = pl.ds(pl.multiple_of((info_ref[0] + 1) * GROUP, GROUP), GROUP)
    block_ref[...] = relu_layers([gram_ref[at, :]], [q_ref[at, :]], tab_ref, 0, PANEL)[0]


def diagonal_kernel(
    info_ref, src_ref, raw_ref, x_ref, block_ref, a_ref, out_ref, all_ref, p_ref, tab_ref, qrow_ref, q_ref, *sems
):
    steps = iter(gather_steps(block_ref, all_ref, *sems))
    step = lambda: next(steps)()
    step()
    place_points(src_ref, raw_ref, p_ref)
    for b in range(STEPS):
        along, down = own_square(p_ref, b * TILE)
        store_columns(tab_ref, b * TILE, along)
        qrow_ref[b * TILE : (b + 1) * TILE, :] = jnp.broadcast_to(down, (TILE, TILE))
    step()
    for b in range(PANEL // 256):
        lo = b * 256
        for c in range(b, PANEL // 256):
            a_ref[lo : lo + 256, c * 256 : (c + 1) * 256] = nt(
                p_ref[lo : lo + 256, :], p_ref[c * 256 : (c + 1) * 256, :]
            )
        if b == 0:
            step()
    step()
    local_products(x_ref, p_ref, q_ref, out_ref)
    step()
    panel, place = info_ref[0], info_ref[1] * GROUP
    all_columns = lax.broadcasted_iota(jnp.int32, (GROUP, PANEL), 1)
    all_within = lax.broadcasted_iota(jnp.int32, (GROUP, PANEL), 0)

    def local_blocks(f, carry):
        rounds = [f * 4 + n for n in range(4)]
        at = [pl.ds(pl.multiple_of(r * GROUP, GROUP), GROUP) for r in rounds]
        k = relu_layers([out_ref[a, :] for a in at], [q_ref[a, :] for a in at], tab_ref, 0, PANEL)
        for r, a, rows in zip(rounds, at, k):
            own = (r == panel) & (all_columns == place + all_within)
            out_ref[a, :] = jnp.where(r >= panel, rows + jnp.where(own, noise_var, 0.0), 0.0)
        return carry

    lax.fori_loop(0, out_ref.shape[0] // 32, local_blocks, 0)
    for b in range(STEPS):
        lo = b * TILE
        width = PANEL - lo
        many = 4 if b < 4 else 8 if b < 7 else 16
        column = lax.broadcasted_iota(jnp.int32, (GROUP, width), 1) + lo
        within = lax.broadcasted_iota(jnp.int32, (GROUP, width), 0)

        def row_blocks(f, carry, lo=lo, width=width, many=many, column=column, within=within):
            starts = [pl.multiple_of(lo + (f * many + n) * GROUP, GROUP) for n in range(many)]
            at = [pl.ds(r, GROUP) for r in starts]
            k = relu_layers([a_ref[a, lo:] for a in at], [qrow_ref[a, :] for a in at], tab_ref, lo, width)
            for r, a, rows in zip(starts, at, k):
                a_ref[a, lo:] = rows + jnp.where(column == r + within, noise_var, 0.0)
            return carry

        lax.fori_loop(0, TILE // GROUP // many, row_blocks, 0)
        if b in (0, 2):
            step()
    step()


def factor_kernel(info_ref, m_ref, k_ref, f_ref, g_ref, a_ref, inv_ref, d_ref, cs_ref):
    a_ref[...] = m_ref[...]
    row = lax.broadcasted_iota(jnp.int32, (TILE, TILE), 0)
    col = lax.broadcasted_iota(jnp.int32, (TILE, TILE), 1)
    f_ref[...] = k_ref[...]

    def step(k, carry):
        k0 = pl.multiple_of(k * TILE, TILE)
        d_ref[...] = a_ref[pl.ds(k0, TILE), pl.ds(k0, TILE)]
        block_inverse(d_ref, cs_ref)
        linv = jnp.where(row >= col, d_ref[...], 0.0)
        inv_ref[k] = linv
        for kk in range(STEPS - 1):

            @pl.when(k == kk)
            def _():
                b0, c0 = kk * TILE, (kk + 1) * TILE
                u = nn(lhs6(linv), rhs6_nn(a_ref[b0:c0, c0:]))
                a_ref[b0:c0, c0:] = u
                u6 = rhs6_nn(u)
                for i in range(kk + 1, STEPS):
                    i0 = i * TILE
                    x = u[:, i0 - c0 : i0 - c0 + TILE].T
                    a_ref[i0 : i0 + TILE, i0:] = a_ref[i0 : i0 + TILE, i0:] - nn(
                        lhs6(x), u6[:, i0 - c0 :]
                    )

        return carry

    lax.fori_loop(0, STEPS, step, 0)

    for k in range(STEPS):
        b0, c0 = k * TILE, (k + 1) * TILE
        x = nt(lhs6(f_ref[:, b0:c0]), rhs6_nt(inv_ref[k]))
        f_ref[:, b0:c0] = x
        if k < STEPS - 1:
            f_ref[:, c0:] = f_ref[:, c0:] - nn(lhs6(x), rhs6_nn(a_ref[b0:c0, c0:]))

    at = pl.ds(pl.multiple_of(info_ref[0] * GROUP, GROUP), GROUP)
    column = lax.broadcasted_iota(jnp.int32, (GROUP, PANEL), 1)
    within = lax.broadcasted_iota(jnp.int32, (GROUP, PANEL), 0)
    f_ref[at, :] = jnp.where(column <= info_ref[1] * GROUP + within, f_ref[at, :], 0.0)

    g_ref[...] = f_ref[...]
    for k in range(STEPS - 1, -1, -1):
        b0, c0 = k * TILE, (k + 1) * TILE
        x = nn(lhs6(g_ref[:, b0:c0]), rhs6_nn(inv_ref[k]))
        g_ref[:, b0:c0] = x
        if k:
            g_ref[:, :b0] = g_ref[:, :b0] - nt(lhs6(x), rhs6_nt(a_ref[:b0, b0:c0]))


def update_kernel(info_ref, src_ref, g_ref, nk_ref, nl_ref, out_ref, kn_ref):
    def place(b, carry):
        at = pl.ds(pl.multiple_of(b * GROUP, GROUP), GROUP)
        kn_ref[at, :] = nk_ref[src_ref[b]]
        return carry

    lax.fori_loop(0, PANEL // GROUP, place, 0, unroll=8)
    rows = lax.broadcasted_iota(jnp.int32, (g_ref.shape[0], 256), 0) // GROUP
    live = rows > info_ref[0]
    for b in range(PANEL // 256):
        total = nl_ref[:, b * 256 : (b + 1) * 256]
        for k in range(STEPS):
            k0 = k * TILE
            total = total - nt(
                lhs6(g_ref[:, k0 : k0 + TILE]),
                rhs6_nt(kn_ref[b * 256 : (b + 1) * 256, k0 : k0 + TILE]),
            )
        out_ref[:, b * 256 : (b + 1) * 256] = jnp.where(live, total, 0.0)


ORDERS = (("x", "y", "z"), ("y", "z", "x"), ("z", "x", "y"))


def gather_steps(block_ref, out_ref, near_send, near_recv, pair_send, pair_recv, own_sem):
    row, sub = lax.axis_index("row"), lax.axis_index("sub")
    me = {"z": row // 8, "y": row // 2 % 4, "x": sub}
    core = row % 2
    width = block_ref.shape[1]
    tiles = width // TILE
    first = [0, (tiles * 3 + 7) // 8, (tiles * 3 + 3) // 4, tiles] if tiles % 3 else [n * tiles // 3 for n in range(4)]
    cuts = [(TILE * a, TILE * ((a + b + 1) // 2), TILE * b) for a, b in zip(first, first[1:])]
    every = pl.ds(0, 4)

    def device(at, core_at):
        return (at["z"] * 8 + at["y"] * 2 + core_at, at["x"])

    def shifted(axis, by):
        return {**me, axis: (me[axis] + by + 4) % 4}

    partner = device(me, 1 - core)
    sent, arriving = [], []

    def part(at, core_at, lo, hi):
        return out_ref.at[at["z"], at["y"], core_at, at["x"], :, lo:hi]

    def copy(src, dst, send, recv, to):
        return pltpu.make_async_remote_copy(
            src_ref=src,
            dst_ref=dst,
            send_sem=send,
            recv_sem=recv,
            device_id=to,
            device_id_type=pl.DeviceIdType.MESH,
        )

    def to_partner(at, lo, hi, slot):
        ours, theirs = part(at, core, lo, hi), part(at, 1 - core, lo, hi)
        c = copy(ours, ours, pair_send.at[slot], pair_recv.at[slot], partner)
        c.start()
        sent.append(c)
        arriving.append(copy(theirs, theirs, pair_send.at[slot], pair_recv.at[slot], partner))

    def sets(s, t, by):
        order = ORDERS[s]
        axis = order[t]
        return {
            **{a: every if order.index(a) < t else me[a] for a in "zyx"},
            axis: (me[axis] + by + 4) % 4,
        }

    def near(s, t, kind, end):
        lo, mid, hi = cuts[s]
        lo, hi = ((lo, hi), (lo, hi), (lo, mid), (mid, hi))[kind]
        to = device(shifted(ORDERS[s][t], 1 if kind in (0, 2) else -1), core)

        def along(by):
            piece = part(sets(s, t, by), core, lo, hi)
            source = block_ref.at[:, lo:hi] if t == 0 and by == 0 else piece
            return copy(source, piece, near_send.at[s, t, kind], near_recv.at[s, t, kind], to)

        return along(((0, 0, -1, 1), (-1, 1, 2, 2))[end][kind])

    def send(s, t, kind):
        c = near(s, t, kind, 0)
        c.start()
        sent.append(c)

    def begin(t):
        for s in range(3):
            send(s, t, 0)
            send(s, t, 1)

    mine = pltpu.make_async_copy(block_ref, part(me, core, 0, width), own_sem)

    def enter():
        peers = [device(shifted(a, by), core) for a in "zyx" for by in (1, -1)] + [partner]
        barrier = pltpu.get_barrier_semaphore()
        for peer in peers:
            pl.semaphore_signal(barrier, inc=1, device_id=peer, device_id_type=pl.DeviceIdType.MESH)
        pl.semaphore_wait(barrier, len(peers))
        mine.start()
        begin(0)

    def pass_on(t):
        if t == 0:
            mine.wait()
            to_partner(me, 0, width, 27)
        for s in range(3):
            for kind in (0, 1):
                near(s, t, kind, 1).wait_recv()
                send(s, t, 2 + kind)
        for s in range(3):
            lo, _, hi = cuts[s]
            to_partner(sets(s, t, -1), lo, hi, 9 * s + 3 * t)
            to_partner(sets(s, t, 1), lo, hi, 9 * s + 3 * t + 1)

    def complete(t):
        for s in range(3):
            for kind in (2, 3):
                near(s, t, kind, 1).wait_recv()
        if t < 2:
            begin(t + 1)
        for s in range(3):
            lo, _, hi = cuts[s]
            to_partner(sets(s, t, 2), lo, hi, 9 * s + 3 * t + 2)

    def leave():
        for c in arriving:
            c.wait_recv()
        for c in sent:
            c.wait_send()

    steps = [enter]
    for t in range(3):
        steps += [lambda t=t: pass_on(t), lambda t=t: complete(t)]
    return steps + [leave]


GATHER_SCRATCH = [
    pltpu.SemaphoreType.DMA((3, 3, 4)),
    pltpu.SemaphoreType.DMA((3, 3, 4)),
    pltpu.SemaphoreType.DMA((28,)),
    pltpu.SemaphoreType.DMA((28,)),
    pltpu.SemaphoreType.DMA,
]


def gather_kernel(*refs):
    for step in gather_steps(*refs):
        step()


def gather_blocks(block, collective_id):
    rows, width = block.shape
    out = pl.pallas_call(
        gather_kernel,
        out_shape=jax.ShapeDtypeStruct((4, 4, 2, 4, rows, width), block.dtype),
        in_specs=[VMEM],
        out_specs=ANY,
        scratch_shapes=GATHER_SCRATCH,
        compiler_params=pltpu.CompilerParams(collective_id=collective_id, has_side_effects=True),
        name="gather_kernel",
    )(block)
    return out.reshape(128, rows, width)


SMEM = pl.BlockSpec(memory_space=pltpu.SMEM)
VMEM = pl.BlockSpec(memory_space=pltpu.VMEM)
ANY = pl.BlockSpec(memory_space=pl.ANY)
PARAMS = pltpu.CompilerParams(vmem_limit_bytes=28 * 1024 * 1024)


def body(images, block_id, panel_index):
    rows_dev, features = images.shape
    shards = lax.axis_size("row") * lax.axis_size("sub")
    myself = lax.axis_index("row") * lax.axis_size("sub") + lax.axis_index("sub")
    panel = panel_index[0]
    everyone = jnp.arange(shards, dtype=jnp.int32)

    def arrangement(which):
        positions = lax.dynamic_index_in_dim(block_id, which, 1, keepdims=False) - which * shards
        sources = jnp.sum(
            jnp.where(positions[None, :] == everyone[:, None], everyone[None, :], 0), axis=1
        )
        return sources, positions[myself]

    def gather(block):
        return lax.all_gather(block, ("row", "sub"), axis=0, tiled=True).reshape(
            shards, GROUP, -1
        )

    def own(which, array):
        return lax.dynamic_slice_in_dim(array, which * GROUP, GROUP, 0)

    sources, position = arrangement(panel)
    next_sources, next_position = arrangement(panel + 1)
    info = jnp.stack([panel, position, next_position])
    points = gather_blocks(own(panel, images), 0)
    next_points = gather(own(panel + 1, images))
    table = pltpu.VMEM((24, PANEL), f32)
    placed = pltpu.VMEM((PANEL, features), bf16)
    rows_out = jax.ShapeDtypeStruct((rows_dev, PANEL), f32)

    local_q = pltpu.VMEM((rows_dev, TILE), f32)
    own_next = pl.pallas_call(
        own_rows_kernel,
        out_shape=jax.ShapeDtypeStruct((GROUP, PANEL), f32),
        in_specs=[SMEM, SMEM, VMEM, VMEM],
        out_specs=VMEM,
        scratch_shapes=[placed, table, local_q, pltpu.VMEM((rows_dev, PANEL), f32)],
        compiler_params=PARAMS,
        name="own_rows_kernel",
        cost_estimate=pl.CostEstimate(flops=10**10, bytes_accessed=16 << 20, transcendentals=0),
    )(info, sources, images, points)
    diagonal, matrix, next_rows = pl.pallas_call(
        diagonal_kernel,
        out_shape=(
            jax.ShapeDtypeStruct((PANEL, PANEL), f32),
            rows_out,
            jax.ShapeDtypeStruct((4, 4, 2, 4, GROUP, PANEL), f32),
        ),
        in_specs=[SMEM, SMEM, VMEM, VMEM, VMEM],
        out_specs=(VMEM, VMEM, ANY),
        scratch_shapes=[placed, table, pltpu.VMEM((PANEL, TILE), f32), local_q] + GATHER_SCRATCH,
        compiler_params=pltpu.CompilerParams(
            vmem_limit_bytes=46 * 1024 * 1024, collective_id=1, has_side_effects=True
        ),
        name="diagonal_kernel",
        cost_estimate=pl.CostEstimate(flops=3 * 10**10, bytes_accessed=16 << 20, transcendentals=0),
    )(info, sources, points, images, own_next)
    next_rows = next_rows.reshape(shards, GROUP, PANEL)
    factor, weights = pl.pallas_call(
        factor_kernel,
        out_shape=(rows_out, rows_out),
        in_specs=[SMEM, VMEM, VMEM],
        out_specs=(VMEM, VMEM),
        scratch_shapes=[
            pltpu.VMEM((PANEL, PANEL), f32),
            pltpu.VMEM((STEPS, TILE, TILE), f32),
            pltpu.VMEM((TILE, TILE), f32),
            pltpu.VMEM((TILE, TILE), f32),
        ],
        compiler_params=PARAMS,
        name="factor_kernel",
        cost_estimate=pl.CostEstimate(flops=10**11, bytes_accessed=16 << 20, transcendentals=0),
    )(info, diagonal, matrix)
    next_matrix = pl.pallas_call(
        cross_kernel,
        out_shape=rows_out,
        in_specs=[SMEM, SMEM, VMEM, VMEM],
        out_specs=VMEM,
        scratch_shapes=[placed, table, local_q],
        compiler_params=PARAMS,
        name="cross_kernel",
        cost_estimate=pl.CostEstimate(flops=2 * 10**10, bytes_accessed=16 << 20, transcendentals=0),
    )(info, next_sources, images, next_points)
    updated = pl.pallas_call(
        update_kernel,
        out_shape=rows_out,
        in_specs=[SMEM, SMEM, VMEM, VMEM, VMEM],
        out_specs=VMEM,
        scratch_shapes=[pltpu.VMEM((PANEL, PANEL), f32)],
        compiler_params=PARAMS,
        name="update_kernel",
        cost_estimate=pl.CostEstimate(flops=10**10, bytes_accessed=16 << 20, transcendentals=0),
    )(info, next_sources, weights, next_rows, next_matrix)
    return (factor, updated)


def solution(mesh):
    in_specs = (P(("row", "sub"), None), P(), P())
    out_specs = (P(("row", "sub"), None), P(("row", "sub"), None))
    return jax.shard_map(body, mesh=mesh, in_specs=in_specs, out_specs=out_specs, check_vma=False)
```

```python
import math

import jax
import jax.numpy as jnp
from jax import lax
from jax.experimental import pallas as pl
from jax.experimental.pallas import tpu as pltpu
from jax.sharding import PartitionSpec as P

PANEL = 1024
DEPTH = 10
GROUP = 8
TILE = 128
STEPS = PANEL // TILE

weight_var = 2.0
bias_var = 0.1
noise_var = 0.1
f32 = jnp.float32
bf16 = jnp.bfloat16

ARC_A = 0.2353731889436501
ARC_B = 0.116208962721599
ARC_C = 3.2233309496295237
ARC_D = 0.005000674198862276


def nn(a, b):
    return lax.dot_general(a, b, (((1,), (0,)), ((), ())), preferred_element_type=f32)


def nt(a, b):
    return lax.dot_general(a, b, (((1,), (1,)), ((), ())), preferred_element_type=f32)


def split3(x):
    h = x.astype(bf16)
    r = x - h.astype(f32)
    m = r.astype(bf16)
    l = (r - m.astype(f32)).astype(bf16)
    return h, m, l


def lhs6(x):
    h, m, l = split3(x)
    return jnp.concatenate([h, m, h, m, h, l], 1)


def rhs6_nn(x):
    h, m, l = split3(x)
    return jnp.concatenate([h, h, m, m, l, h], 0)


def rhs6_nt(x):
    h, m, l = split3(x)
    return jnp.concatenate([h, h, m, m, l, h], 1)


def own_square(rows_ref, start):
    rows = rows_ref[start : start + TILE, :]
    gram = nt(rows, rows)
    eye = lax.broadcasted_iota(jnp.int32, (TILE, TILE), 0) == lax.broadcasted_iota(
        jnp.int32, (TILE, TILE), 1
    )
    only = jnp.where(eye, gram, 0.0)
    scale = weight_var / rows_ref.shape[1]
    return (
        jnp.sum(only, axis=0, keepdims=True) * scale + bias_var,
        jnp.sum(only, axis=1, keepdims=True) * scale + bias_var,
    )


def layer_scales(q):
    inv = [lax.rsqrt(q + bias_var * n) for n in range(DEPTH)]
    ratio = [(q + bias_var * n) * inv[n] * inv[n + 1] for n in range(DEPTH - 1)]
    offset = [inv[n + 1] * math.sqrt(bias_var) for n in range(DEPTH - 1)]
    last = (q + bias_var * (DEPTH - 1)) * inv[DEPTH - 1]
    return inv[0], ratio, offset, last


def store_columns(tab_ref, start, q):
    first, ratio, offset, last = layer_scales(q)
    for at, row in enumerate([first] + ratio + offset + [last]):
        tab_ref[at : at + 1, start : start + TILE] = row


def relu_layers(gram, q_rows, tab_ref, lo, width):
    scales = [layer_scales(q) for q in q_rows]
    pieces = range(width // TILE)
    col = lambda at, w: jnp.broadcast_to(
        tab_ref[at : at + 1, lo + w * TILE : lo + (w + 1) * TILE], (GROUP, TILE)
    )
    scale = weight_var / 3072
    c = [
        [
            (g[:, w * TILE : (w + 1) * TILE] * scale + bias_var) * (first * col(0, w))
            for w in pieces
        ]
        for g, (first, _, _, _) in zip(gram, scales)
    ]
    for n in range(DEPTH):
        for r, (_, ratio, offset, last) in enumerate(scales):
            for w in pieces:
                x = c[r][w]
                u = jnp.maximum(1.0 - (jnp.abs(x) if n == 0 else x), 1e-30)
                p = (ARC_D * u + ARC_A) + ARC_B * lax.rsqrt(ARC_C - u)
                g = (jnp.maximum(x, 0.0) if n == 0 else x) + (u * u) * lax.rsqrt(u) * p
                if n < DEPTH - 1:
                    c[r][w] = g * (ratio[n] * col(1 + n, w)) + offset[n] * col(DEPTH + n, w)
                else:
                    c[r][w] = g * (last * col(2 * DEPTH - 1, w)) + bias_var
    return [jnp.concatenate(row, axis=1) for row in c]


def total(xs):
    xs = list(xs)
    while len(xs) > 1:
        xs = [xs[i] + xs[i + 1] if i + 1 < len(xs) else xs[i] for i in range(0, len(xs), 2)]
    return xs[0]


def block_inverse(d_ref, cs_ref):
    lane = lax.broadcasted_iota(jnp.int32, (8, TILE), 1)
    sub = lax.broadcasted_iota(jnp.int32, (8, TILE), 0)
    spread = lambda x: jnp.broadcast_to(x, (8, TILE))
    now = d_ref[0:8, :]
    for s in range(TILE // 8):
        r0 = 8 * s
        slot = 64 * (s % 2)
        inside = (lane >= r0) & (lane < r0 + 8)
        for j in range(8):
            cs_ref[slot + 8 * j : slot + 8 * j + 8, :] = spread(now[:, r0 + j : r0 + j + 1])
        e = [
            [
                spread(cs_ref[slot + 8 * j + i : slot + 8 * j + i + 1, :]) if j >= i else None
                for j in range(8)
            ]
            for i in range(8)
        ]
        below = {}
        for i in range(s + 1, TILE // 8):
            b = d_ref[8 * i : 8 * i + 8, :]
            below[i] = (b, [spread(b[:, r0 + j : r0 + j + 1]) for j in range(8)])
        t = [
            jnp.where(inside, (lane == r0 + j).astype(f32), spread(d_ref[r0 + j : r0 + j + 1, :]))
            for j in range(8)
        ]
        w = [[None] * 8 for _ in range(8)]
        z = [None] * 8
        rows = [None] * 8
        for j in range(0, 8, 2):
            a, b, c = e[j][j], e[j][j + 1], e[j + 1][j + 1]
            root_det = lax.rsqrt(a * c - b * b)
            root_a = lax.rsqrt(a)
            rd = root_det * root_det
            for i in range(j + 2, 8):
                f0 = (c * e[j][i] - b * e[j + 1][i]) * rd
                f1 = (a * e[j + 1][i] - b * e[j][i]) * rd
                for q in range(i, 8):
                    e[i][q] = e[i][q] - (f0 * e[j][q] + f1 * e[j + 1][q])
                t[i] = t[i] - (f0 * t[j] + f1 * t[j + 1])
                for k in range(j):
                    w[i][k] = w[i][k] - (f0 * w[j][k] + f1 * w[j + 1][k])
                w[i][j], w[i][j + 1] = -f0, -f1
            z[j] = (c * t[j] - b * t[j + 1]) * rd
            z[j + 1] = (a * t[j + 1] - b * t[j]) * rd
            rows[j] = t[j] * root_a
            rows[j + 1] = (t[j + 1] - (b * (root_a * root_a)) * t[j]) * (root_det * (a * root_a))
        g = [total([z[k]] + [w[i][k] * z[i] for i in range(k // 2 * 2 + 2, 8)]) for k in range(8)]
        out = rows[7]
        for j in range(6, -1, -1):
            out = jnp.where(sub == j, rows[j], out)
        d_ref[r0 : r0 + 8, :] = out
        for i in range(s + 1, TILE // 8):
            b, c = below[i]
            acc = jnp.where(inside, 0.0, b) - total([c[j] * g[j] for j in range(8)])
            d_ref[8 * i : 8 * i + 8, :] = acc
            if i == s + 1:
                now = acc


def place_points(src_ref, raw_ref, p_ref):
    def place(b, carry):
        pair = [raw_ref[src_ref[2 * b + n]].astype(f32) for n in range(2)]
        at = pl.ds(pl.multiple_of(b * 2 * GROUP, 2 * GROUP), 2 * GROUP)
        p_ref[at, :] = jnp.concatenate(pair, axis=0).astype(bf16)
        return carry

    lax.fori_loop(0, PANEL // (2 * GROUP), place, 0)


def local_kernel(info_ref, x_ref, q_ref, p_ref, out_ref, tab_ref, after):
    for b in range(x_ref.shape[0] // TILE):
        down = own_square(x_ref, b * TILE)[1]
        q_ref[b * TILE : (b + 1) * TILE, :] = jnp.broadcast_to(down, (TILE, TILE))
    for b in range(PANEL // 256):
        out_ref[:, b * 256 : (b + 1) * 256] = nt(x_ref[...], p_ref[b * 256 : (b + 1) * 256, :])
    start = info_ref[0] + after
    place = info_ref[1 + after] * GROUP
    column = lax.broadcasted_iota(jnp.int32, (GROUP, PANEL), 1)
    within = lax.broadcasted_iota(jnp.int32, (GROUP, PANEL), 0)

    def row_blocks(f, carry):
        rounds = [f * 4 + n for n in range(4)]
        at = [pl.ds(pl.multiple_of(r * GROUP, GROUP), GROUP) for r in rounds]
        k = relu_layers([out_ref[a, :] for a in at], [q_ref[a, :] for a in at], tab_ref, 0, PANEL)
        for r, a, rows in zip(rounds, at, k):
            own = (r == start) & (column == place + within)
            out_ref[a, :] = jnp.where(r >= start, rows + jnp.where(own, noise_var, 0.0), 0.0)
        return carry

    def clear(f, carry):
        out_ref[pl.ds(pl.multiple_of(f * 32, 32), 32), :] = jnp.zeros((32, PANEL), f32)
        return carry

    lax.fori_loop(0, start // 4, clear, 0)
    lax.fori_loop(start // 4, out_ref.shape[0] // 32, row_blocks, 0)


def cross_kernel(info_ref, src_ref, x_ref, raw_ref, out_ref, *refs, after):
    block_ref, p_ref, tab_ref, q_ref = refs if after == 0 else (None, *refs)
    place_points(src_ref, raw_ref, p_ref)
    for b in range(STEPS):
        store_columns(tab_ref, b * TILE, own_square(p_ref, b * TILE)[0])
    local_kernel(info_ref, x_ref, q_ref, p_ref, out_ref, tab_ref, after)
    if after == 0:
        at = pl.multiple_of((info_ref[0] + 1) * GROUP, GROUP)
        block_ref[...] = out_ref[pl.ds(at, GROUP), :]


def diagonal_kernel(src_ref, raw_ref, block_ref, a_ref, all_ref, p_ref, tab_ref, qrow_ref, *sems):
    steps = iter(gather_steps(block_ref, all_ref, *sems))
    step = lambda: next(steps)()
    step()
    place_points(src_ref, raw_ref, p_ref)
    step()
    for b in range(STEPS):
        along, down = own_square(p_ref, b * TILE)
        store_columns(tab_ref, b * TILE, along)
        qrow_ref[b * TILE : (b + 1) * TILE, :] = jnp.broadcast_to(down, (TILE, TILE))
    step()
    for b in range(PANEL // 256):
        lo = b * 256
        for c in range(b, PANEL // 256):
            a_ref[lo : lo + 256, c * 256 : (c + 1) * 256] = nt(
                p_ref[lo : lo + 256, :], p_ref[c * 256 : (c + 1) * 256, :]
            )
        if b in (0, 3):
            step()
    for b in range(STEPS):
        lo = b * TILE
        width = PANEL - lo
        many = 4 if b < 4 else 8 if b < 7 else 16
        column = lax.broadcasted_iota(jnp.int32, (GROUP, width), 1) + lo
        within = lax.broadcasted_iota(jnp.int32, (GROUP, width), 0)

        def row_blocks(f, carry, lo=lo, width=width, many=many, column=column, within=within):
            starts = [pl.multiple_of(lo + (f * many + n) * GROUP, GROUP) for n in range(many)]
            at = [pl.ds(r, GROUP) for r in starts]
            k = relu_layers([a_ref[a, lo:] for a in at], [qrow_ref[a, :] for a in at], tab_ref, lo, width)
            for r, a, rows in zip(starts, at, k):
                a_ref[a, lo:] = rows + jnp.where(column == r + within, noise_var, 0.0)
            return carry

        lax.fori_loop(0, TILE // GROUP // many, row_blocks, 0)
        if b in (1, 3):
            step()
    step()


def factor_kernel(info_ref, m_ref, k_ref, f_ref, g_ref, a_ref, inv_ref, d_ref, cs_ref):
    a_ref[...] = m_ref[...]
    row = lax.broadcasted_iota(jnp.int32, (TILE, TILE), 0)
    col = lax.broadcasted_iota(jnp.int32, (TILE, TILE), 1)
    f_ref[...] = k_ref[...]

    def step(k, carry):
        k0 = pl.multiple_of(k * TILE, TILE)
        d_ref[...] = a_ref[pl.ds(k0, TILE), pl.ds(k0, TILE)]
        block_inverse(d_ref, cs_ref)
        linv = jnp.where(row >= col, d_ref[...], 0.0)
        inv_ref[k] = linv
        for kk in range(STEPS - 1):

            @pl.when(k == kk)
            def _():
                b0, c0 = kk * TILE, (kk + 1) * TILE
                u = nn(lhs6(linv), rhs6_nn(a_ref[b0:c0, c0:]))
                a_ref[b0:c0, c0:] = u
                u6 = rhs6_nn(u)
                for i in range(kk + 1, STEPS):
                    i0 = i * TILE
                    x = u[:, i0 - c0 : i0 - c0 + TILE].T
                    a_ref[i0 : i0 + TILE, i0:] = a_ref[i0 : i0 + TILE, i0:] - nn(
                        lhs6(x), u6[:, i0 - c0 :]
                    )

        return carry

    lax.fori_loop(0, STEPS, step, 0)

    for k in range(STEPS):
        b0, c0 = k * TILE, (k + 1) * TILE
        x = nt(lhs6(f_ref[:, b0:c0]), rhs6_nt(inv_ref[k]))
        f_ref[:, b0:c0] = x
        if k < STEPS - 1:
            f_ref[:, c0:] = f_ref[:, c0:] - nn(lhs6(x), rhs6_nn(a_ref[b0:c0, c0:]))

    at = pl.ds(pl.multiple_of(info_ref[0] * GROUP, GROUP), GROUP)
    column = lax.broadcasted_iota(jnp.int32, (GROUP, PANEL), 1)
    within = lax.broadcasted_iota(jnp.int32, (GROUP, PANEL), 0)
    f_ref[at, :] = jnp.where(column <= info_ref[1] * GROUP + within, f_ref[at, :], 0.0)

    g_ref[...] = f_ref[...]
    for k in range(STEPS - 1, -1, -1):
        b0, c0 = k * TILE, (k + 1) * TILE
        x = nn(lhs6(g_ref[:, b0:c0]), rhs6_nn(inv_ref[k]))
        g_ref[:, b0:c0] = x
        if k:
            g_ref[:, :b0] = g_ref[:, :b0] - nt(lhs6(x), rhs6_nt(a_ref[:b0, b0:c0]))


def update_kernel(info_ref, src_ref, g_ref, nk_ref, nl_ref, out_ref, kn_ref):
    def place(b, carry):
        at = pl.ds(pl.multiple_of(b * GROUP, GROUP), GROUP)
        kn_ref[at, :] = nk_ref[src_ref[b]]
        return carry

    lax.fori_loop(0, PANEL // GROUP, place, 0, unroll=8)
    rows = lax.broadcasted_iota(jnp.int32, (g_ref.shape[0], 256), 0) // GROUP
    live = rows > info_ref[0]
    for b in range(PANEL // 256):
        total = nl_ref[:, b * 256 : (b + 1) * 256]
        for k in range(STEPS):
            k0 = k * TILE
            total = total - nt(
                lhs6(g_ref[:, k0 : k0 + TILE]),
                rhs6_nt(kn_ref[b * 256 : (b + 1) * 256, k0 : k0 + TILE]),
            )
        out_ref[:, b * 256 : (b + 1) * 256] = jnp.where(live, total, 0.0)


ORDERS = (("x", "y", "z"), ("y", "z", "x"), ("z", "x", "y"))


def gather_steps(block_ref, out_ref, near_send, near_recv, pair_send, pair_recv, own_sem):
    row, sub = lax.axis_index("row"), lax.axis_index("sub")
    me = {"z": row // 8, "y": row // 2 % 4, "x": sub}
    core = row % 2
    width = block_ref.shape[1]
    tiles = width // TILE
    first = [0, (tiles * 3 + 7) // 8, (tiles * 3 + 3) // 4, tiles] if tiles % 3 else [n * tiles // 3 for n in range(4)]
    cuts = [(TILE * a, TILE * ((a + b + 1) // 2), TILE * b) for a, b in zip(first, first[1:])]
    every = pl.ds(0, 4)

    def device(at, core_at):
        return (at["z"] * 8 + at["y"] * 2 + core_at, at["x"])

    def shifted(axis, by):
        return {**me, axis: (me[axis] + by + 4) % 4}

    partner = device(me, 1 - core)
    sent, arriving = [], []

    def part(at, core_at, lo, hi):
        return out_ref.at[at["z"], at["y"], core_at, at["x"], :, lo:hi]

    def copy(src, dst, send, recv, to):
        return pltpu.make_async_remote_copy(
            src_ref=src,
            dst_ref=dst,
            send_sem=send,
            recv_sem=recv,
            device_id=to,
            device_id_type=pl.DeviceIdType.MESH,
        )

    def to_partner(at, lo, hi, slot):
        ours, theirs = part(at, core, lo, hi), part(at, 1 - core, lo, hi)
        c = copy(ours, ours, pair_send.at[slot], pair_recv.at[slot], partner)
        c.start()
        sent.append(c)
        arriving.append(copy(theirs, theirs, pair_send.at[slot], pair_recv.at[slot], partner))

    def sets(s, t, by):
        order = ORDERS[s]
        axis = order[t]
        return {
            **{a: every if order.index(a) < t else me[a] for a in "zyx"},
            axis: (me[axis] + by + 4) % 4,
        }

    def near(s, t, kind, end):
        lo, mid, hi = cuts[s]
        lo, hi = ((lo, hi), (lo, hi), (lo, mid), (mid, hi))[kind]
        to = device(shifted(ORDERS[s][t], 1 if kind in (0, 2) else -1), core)

        def along(by):
            piece = part(sets(s, t, by), core, lo, hi)
            source = block_ref.at[:, lo:hi] if t == 0 and by == 0 else piece
            return copy(source, piece, near_send.at[s, t, kind], near_recv.at[s, t, kind], to)

        return along(((0, 0, -1, 1), (-1, 1, 2, 2))[end][kind])

    def send(s, t, kind):
        c = near(s, t, kind, 0)
        c.start()
        sent.append(c)

    def begin(t):
        for s in range(3):
            send(s, t, 0)
            send(s, t, 1)

    mine = pltpu.make_async_copy(block_ref, part(me, core, 0, width), own_sem)

    def enter():
        peers = [device(shifted(a, by), core) for a in "zyx" for by in (1, -1)] + [partner]
        barrier = pltpu.get_barrier_semaphore()
        for peer in peers:
            pl.semaphore_signal(barrier, inc=1, device_id=peer, device_id_type=pl.DeviceIdType.MESH)
        pl.semaphore_wait(barrier, len(peers))
        mine.start()
        begin(0)

    def pass_on(t):
        if t == 0:
            mine.wait()
            to_partner(me, 0, width, 27)
        for s in range(3):
            for kind in (0, 1):
                near(s, t, kind, 1).wait_recv()
                send(s, t, 2 + kind)
        for s in range(3):
            lo, _, hi = cuts[s]
            to_partner(sets(s, t, -1), lo, hi, 9 * s + 3 * t)
            to_partner(sets(s, t, 1), lo, hi, 9 * s + 3 * t + 1)

    def complete(t):
        for s in range(3):
            for kind in (2, 3):
                near(s, t, kind, 1).wait_recv()
        if t < 2:
            begin(t + 1)
        for s in range(3):
            lo, _, hi = cuts[s]
            to_partner(sets(s, t, 2), lo, hi, 9 * s + 3 * t + 2)

    def leave():
        for c in arriving:
            c.wait_recv()
        for c in sent:
            c.wait_send()

    steps = [enter]
    for t in range(3):
        steps += [lambda t=t: pass_on(t), lambda t=t: complete(t)]
    return steps + [leave]


GATHER_SCRATCH = [
    pltpu.SemaphoreType.DMA((3, 3, 4)),
    pltpu.SemaphoreType.DMA((3, 3, 4)),
    pltpu.SemaphoreType.DMA((28,)),
    pltpu.SemaphoreType.DMA((28,)),
    pltpu.SemaphoreType.DMA,
]


def gather_kernel(*refs):
    for step in gather_steps(*refs):
        step()


def gather_blocks(block, collective_id):
    rows, width = block.shape
    out = pl.pallas_call(
        gather_kernel,
        out_shape=jax.ShapeDtypeStruct((4, 4, 2, 4, rows, width), block.dtype),
        in_specs=[VMEM],
        out_specs=ANY,
        scratch_shapes=GATHER_SCRATCH,
        compiler_params=pltpu.CompilerParams(collective_id=collective_id, has_side_effects=True),
        name="gather_kernel",
    )(block)
    return out.reshape(128, rows, width)


SMEM = pl.BlockSpec(memory_space=pltpu.SMEM)
VMEM = pl.BlockSpec(memory_space=pltpu.VMEM)
ANY = pl.BlockSpec(memory_space=pl.ANY)
PARAMS = pltpu.CompilerParams(vmem_limit_bytes=28 * 1024 * 1024)


def body(images, block_id, panel_index):
    rows_dev, features = images.shape
    shards = lax.axis_size("row") * lax.axis_size("sub")
    myself = lax.axis_index("row") * lax.axis_size("sub") + lax.axis_index("sub")
    panel = panel_index[0]
    everyone = jnp.arange(shards, dtype=jnp.int32)

    def arrangement(which):
        positions = lax.dynamic_index_in_dim(block_id, which, 1, keepdims=False) - which * shards
        sources = jnp.sum(
            jnp.where(positions[None, :] == everyone[:, None], everyone[None, :], 0), axis=1
        )
        return sources, positions[myself]

    def gather(block):
        return lax.all_gather(block, ("row", "sub"), axis=0, tiled=True).reshape(
            shards, GROUP, -1
        )

    def own(which, array):
        return lax.dynamic_slice_in_dim(array, which * GROUP, GROUP, 0)

    sources, position = arrangement(panel)
    next_sources, next_position = arrangement(panel + 1)
    info = jnp.stack([panel, position, next_position])
    points = gather_blocks(own(panel, images), 0)
    next_points = gather(own(panel + 1, images))
    table = pltpu.VMEM((24, PANEL), f32)
    placed = pltpu.VMEM((PANEL, features), bf16)
    rows_out = jax.ShapeDtypeStruct((rows_dev, PANEL), f32)

    def cross(blocks, order, after):
        return pl.pallas_call(
            lambda *refs: cross_kernel(*refs, after=after),
            out_shape=rows_out if after else (rows_out, jax.ShapeDtypeStruct((GROUP, PANEL), f32)),
            in_specs=[SMEM, SMEM, VMEM, VMEM],
            out_specs=VMEM if after else (VMEM, VMEM),
            scratch_shapes=[placed, table, pltpu.VMEM((rows_dev, TILE), f32)],
            compiler_params=PARAMS,
            name="cross_kernel",
            cost_estimate=pl.CostEstimate(flops=2 * 10**10, bytes_accessed=16 << 20, transcendentals=0),
        )(info, order, images, blocks)

    matrix, own_next = cross(points, sources, 0)
    diagonal, next_rows = pl.pallas_call(
        diagonal_kernel,
        out_shape=(
            jax.ShapeDtypeStruct((PANEL, PANEL), f32),
            jax.ShapeDtypeStruct((4, 4, 2, 4, GROUP, PANEL), f32),
        ),
        in_specs=[SMEM, VMEM, VMEM],
        out_specs=(VMEM, ANY),
        scratch_shapes=[placed, table, pltpu.VMEM((PANEL, TILE), f32)] + GATHER_SCRATCH,
        compiler_params=pltpu.CompilerParams(
            vmem_limit_bytes=48 * 1024 * 1024, collective_id=1, has_side_effects=True
        ),
        name="diagonal_kernel",
        cost_estimate=pl.CostEstimate(flops=3 * 10**10, bytes_accessed=16 << 20, transcendentals=0),
    )(sources, points, own_next)
    next_rows = next_rows.reshape(shards, GROUP, PANEL)
    factor, weights = pl.pallas_call(
        factor_kernel,
        out_shape=(rows_out, rows_out),
        in_specs=[SMEM, VMEM, VMEM],
        out_specs=(VMEM, VMEM),
        scratch_shapes=[
            pltpu.VMEM((PANEL, PANEL), f32),
            pltpu.VMEM((STEPS, TILE, TILE), f32),
            pltpu.VMEM((TILE, TILE), f32),
            pltpu.VMEM((TILE, TILE), f32),
        ],
        compiler_params=PARAMS,
        name="factor_kernel",
        cost_estimate=pl.CostEstimate(flops=10**11, bytes_accessed=16 << 20, transcendentals=0),
    )(info, diagonal, matrix)
    next_matrix = cross(next_points, next_sources, 1)
    updated = pl.pallas_call(
        update_kernel,
        out_shape=rows_out,
        in_specs=[SMEM, SMEM, VMEM, VMEM, VMEM],
        out_specs=VMEM,
        scratch_shapes=[pltpu.VMEM((PANEL, PANEL), f32)],
        compiler_params=PARAMS,
        name="update_kernel",
        cost_estimate=pl.CostEstimate(flops=10**10, bytes_accessed=16 << 20, transcendentals=0),
    )(info, next_sources, weights, next_rows, next_matrix)
    return (factor, updated)


def solution(mesh):
    in_specs = (P(("row", "sub"), None), P(), P())
    out_specs = (P(("row", "sub"), None), P(("row", "sub"), None))
    return jax.shard_map(body, mesh=mesh, in_specs=in_specs, out_specs=out_specs, check_vma=False)
```
